128 devices in a mesh: seq: 16 (over y, z), rep: 8 (over x, core).
Axes of the slice: x: 4, y: 4, z: 4, core: 2. Of those that a mesh axis runs over, the one named last changes fastest.
Arguments:
- mixed: bfloat16 [8, 16, 512, 2048], P('rep', None, None, 'seq'), may hold values from -6 to 6
- decay_in: bfloat16 [8, 16, 2, 2048], P('rep', None, None, 'seq'), may hold values from -6 to 26.6
- beta_in: bfloat16 [8, 16, 2, 2048], P('rep', None, None, 'seq'), may hold values from -6 to 6
- gate_z: bfloat16 [8, 16, 256, 2048], P('rep', None, None, 'seq'), may hold values from -6 to 6
- conv_weight: bfloat16 [4, 16, 512], P(None, 'seq'), may hold values from -3 to 3
- a_log: float32 [32], P('seq'), may hold values from -10 to 3
- dt_bias: float32 [32], P('seq'), may hold values from -5.5 to -3.5
- norm_gain: float32 [128], replicated, may hold values from 0.5 to 1.5
- req_blocks: int32 [8, 8], P('rep'), may hold values from 1 to 8, 32 in all within a row
- replica_of: int32 [8, 8], P('rep'), may hold values from 0 to 7, as said below
- finished: int32 [8, 8], P('rep'), may hold values from 0 to 1
Outputs:
- mixer_out: bfloat16 [8, 16, 256, 2048], P('rep', None, None, 'seq')
- states_out: float32 [8, 16, 32, 128, 128], P('rep', None, 'seq')
- tails_out: bfloat16 [8, 16, 3, 16, 512], P('rep', None, None, 'seq')
The draws below stay inside these ranges and needn't reach their ends.
Inputs may be any that keep to these rules, and one draw needn't show every extreme that they name: `req_blocks`: blocks of 64 tokens of each of the 8 requests of a pack; together they fill the pack. `replica_of`: at most 2 finished requests of one pack, and at most 16 finished requests of all packs together, name the same replica.
All inputs are finite; a program needn't handle non-finite values.
Results may differ from the reference program's by a relative error of at most 0.012.
Values may be sent and summed in bfloat16 or wider, within the bound.
A program may use at most 64 MiB of HBM per device.

```python
import math
import jax
import jax.numpy as jnp
import numpy as np
from jax import lax

HK = 16
HV = 32
DK = 128
DV = 128
KERNEL = 4
SPAN = 64
REQS = 8
CAP = 2
RATIO = 2
GROUP_CH = 512
SEQ_LEN = 2048
NBLOCKS = 32
MOST_BLOCKS = 8
SLOTS = 16
N_REP = 8


def draw_a_log(key, part):
    linked_tokens = MOST_BLOCKS * SPAN
    pick_key, slow_key, fast_key = jax.random.split(jax.random.fold_in(key, 11), 3)
    quick = jax.random.uniform(pick_key, (HV,)) < 0.5
    slow_rate = jax.random.uniform(slow_key, (HV,), minval=0.25, maxval=1.0) / (0.05 * linked_tokens)
    fast_rate = jnp.exp(jax.random.uniform(fast_key, (HV,), minval=jnp.log(2.0), maxval=jnp.log(8.0)))
    return jnp.log(jnp.where(quick, fast_rate, slow_rate)).astype(jnp.float32)


def draw_decay_in(key, part):
    linked_tokens = MOST_BLOCKS * SPAN
    full_shape = (N_REP, HK, RATIO, SEQ_LEN)
    base_key, random_spot_key, height_key = jax.random.split(jax.random.fold_in(key, 13), 3)
    base_offset = jnp.clip(jax.random.normal(base_key, full_shape), -6.0, 6.0)
    request_runs = jax.random.uniform(random_spot_key, full_shape) < 3.0 / linked_tokens
    block_height = jax.random.uniform(height_key, full_shape, minval=0.02, maxval=0.05) * linked_tokens
    return jnp.where(request_runs, block_height, base_offset).astype(jnp.float32).astype(jnp.bfloat16)


def replica_table(key):
    busy_key, pair_key, offset_key, done_key, order_key = jax.random.split(jax.random.fold_in(key, 7), 5)
    pair_count = REQS // CAP
    busy = jax.random.randint(busy_key, (), 0, N_REP)
    busy_pair = jax.random.randint(pair_key, (N_REP, 1), 0, pair_count)
    offsets = jax.random.randint(offset_key, (N_REP, 1), 0, N_REP - 1)
    request_index = jnp.arange(REQS, dtype=jnp.int32)[None, :]
    pair_index = request_index // CAP
    other_index = pair_index - (pair_index > busy_pair).astype(jnp.int32)
    other_dest = (busy + 1 + (offsets + other_index) % (N_REP - 1)) % N_REP
    dest = jnp.where(pair_index == busy_pair, busy, other_dest).astype(jnp.int32)
    coin = (jax.random.randint(done_key, (N_REP, REQS), 0, 4) > 0).astype(jnp.int32)
    done = jnp.where(pair_index == busy_pair, 1, coin).astype(jnp.int32)
    orders = jax.vmap(lambda one_key: jax.random.permutation(one_key, REQS))(jax.random.split(order_key, N_REP))
    dest = jnp.take_along_axis(dest, orders, axis=1)
    done = jnp.take_along_axis(done, orders, axis=1)
    return (dest.astype(jnp.int32), done.astype(jnp.int32))


def draw_replica_of(key, part):
    dest, done = replica_table(key)
    return dest


def draw_finished(key, part):
    dest, done = replica_table(key)
    return done


def block_scale(key, dims, shards, low, top_value):
    factor_of, own = 1.0, jax.random.fold_in(key, 6)
    for dim, blocks in shards:
        heights = jnp.exp(jax.random.uniform(jax.random.fold_in(own, dim), (blocks,), jnp.float32, low / len(shards), top_value / len(shards)))
        factor_of = factor_of * jnp.repeat(heights, dims[dim] // blocks).reshape([-1 if axis == dim else 1 for axis in range(len(dims))])
    return factor_of


def profile(count, total, bound, lean):
    loads = [(1 << 20) // math.isqrt(rank ** lean) + 1 for rank in range(2, count + 1)]
    surplus, counts = total - bound - (count - 1), [1] * (count - 1)
    while surplus > 0:
        free = [i for i in range(count - 1) if counts[i] < bound]
        whole, remaining = sum([loads[i] for i in free]), surplus
        for i in free:
            extra = min(bound - counts[i], max(1, remaining * loads[i] // whole), surplus)
            counts[i] = counts[i] + extra
            surplus = surplus - extra
    return np.array([bound] + counts)


def uneven_parts(stream_key, count, total, limit, skew):
    if count == 2:
        one = jax.random.randint(stream_key, (), max(1, total - limit), min(limit, total - 1) + 1)
        return jnp.stack([one, total - one])
    tallies = jnp.asarray(profile(count, total, limit, skew), jnp.int32)
    twos = (count - 1) // 2
    donor, receiver = tallies[1:1 + 2 * twos:2], tallies[2:2 + 2 * twos:2]
    slack = jnp.minimum(donor - 1, limit - receiver)
    shifted = jax.random.randint(jax.random.fold_in(stream_key, 1), (twos,), 0, 1 << 20) % (slack + 1)
    tallies = tallies.at[1:1 + 2 * twos:2].set(donor - shifted).at[2:2 + 2 * twos:2].set(receiver + shifted)
    return tallies[jax.random.permutation(jax.random.fold_in(stream_key, 2), count)]


def noise(key, extent, scale, most, cuts=(), kind=jnp.bfloat16):
    array = scale * jax.random.normal(key, extent, jnp.float32)
    if cuts:
        array = array * block_scale(key, extent, cuts, -0.22, 0.18)
    return jnp.clip(array, -most, most).astype(kind)


def setup_inputs(seed: int = 0) -> dict:
    seeds = jax.random.split(jax.random.key(seed), 12)
    return {
        "mixed": noise(seeds[0], (N_REP, HK, GROUP_CH, SEQ_LEN), 1.0, 6.0, ((0, 8), (3, 16))),
        "decay_in": draw_decay_in(jax.random.fold_in(seeds[11], 71), 0),
        "beta_in": noise(seeds[2], (N_REP, HK, RATIO, SEQ_LEN), 1.5, 6.0, ((0, 8), (3, 16))),
        "gate_z": noise(seeds[3], (N_REP, HK, RATIO * DV, SEQ_LEN), 1.0, 6.0, ((0, 8), (3, 16))),
        "conv_weight": noise(seeds[4], (KERNEL, HK, GROUP_CH), KERNEL ** -0.5, 3.0, ((1, 16),)),
        "a_log": draw_a_log(jax.random.fold_in(seeds[11], 71), 0),
        "dt_bias": jnp.clip(-5.5 + 2.0 * jax.random.uniform(seeds[6], (HV,), jnp.float32) ** block_scale(seeds[6], (HV,), ((0, 16),), -0.2, 0.2), -5.5, -3.5),
        "norm_gain": jnp.clip(1.0 + 0.1 * jax.random.normal(seeds[7], (DV,), jnp.float32), 0.5, 1.5),
        "req_blocks": jax.vmap(lambda own: uneven_parts(own, REQS, NBLOCKS, MOST_BLOCKS, 2))(jax.random.split(seeds[8], N_REP)).reshape((N_REP, REQS)).astype(jnp.int32),
        "replica_of": draw_replica_of(jax.random.fold_in(seeds[11], 71), 0),
        "finished": draw_finished(jax.random.fold_in(seeds[11], 71), 0),
    }


EPSILON = 1e-06

def product(spec, left, right):
    return jnp.einsum(spec, left.astype(jnp.float32), right.astype(jnp.float32), precision=lax.Precision.HIGHEST)

def request_bounds(blocks, length):
    block_ends = jnp.cumsum(blocks).astype(jnp.int32)
    block_starts = block_ends - blocks
    start_tokens = block_starts * SPAN
    position = jnp.arange(length, dtype=jnp.int32)
    begins = lax.optimization_barrier(jnp.max(jnp.where(start_tokens[None, :] <= position[:, None], start_tokens[None, :], 0), axis=1))
    first_block = jnp.any(block_starts[None, :] == jnp.arange(length // SPAN, dtype=jnp.int32)[:, None], axis=1)
    return (begins, block_ends * SPAN, first_block, block_ends - 1)

def causal_conv(pre_conv, conv_weight, begins):
    length = pre_conv.shape[-1]
    position = jnp.arange(length, dtype=jnp.int32)
    widened = pre_conv.astype(jnp.float32)
    total = jnp.zeros(pre_conv.shape, jnp.float32)
    for tap_index in range(KERNEL):
        offset_back = KERNEL - 1 - tap_index
        moved = jnp.pad(widened, ((0, 0), (0, 0), (offset_back, 0)))[:, :, :length]
        allowed = position - offset_back >= begins
        total = total + conv_weight[tap_index].astype(jnp.float32)[:, :, None] * jnp.where(allowed[None, None, :], moved, 0.0)
    return jax.nn.silu(total).astype(jnp.bfloat16)

def unit_inverse(mixing):
    minus = -mixing
    total = jnp.eye(SPAN, dtype=jnp.float32) + minus
    power = minus
    for level in range(SPAN.bit_length() - 2):
        power = jnp.matmul(power, power, precision=lax.Precision.HIGHEST)
        total = total + jnp.matmul(total, power, precision=lax.Precision.HIGHEST)
    return total

def delta_heads(convolved, decay_part, beta_part, a_log, dt_bias, first_block):
    head_count, channels, length = convolved.shape
    ratio_count = decay_part.shape[1]
    blocks_total = length // SPAN
    queries = convolved[:, :DK].reshape(head_count, DK, blocks_total, SPAN)
    key_wide = convolved[:, DK:2 * DK].astype(jnp.float32)
    keys_norm = (key_wide * lax.rsqrt(lax.optimization_barrier(jnp.sum(key_wide * key_wide, axis=1, keepdims=True)) + EPSILON)).astype(jnp.bfloat16)
    keys_norm = keys_norm.reshape(head_count, DK, blocks_total, SPAN)
    values_in = convolved[:, 2 * DK:].reshape(head_count, ratio_count, DV, blocks_total, SPAN)
    rates = jnp.exp(a_log).reshape(head_count, ratio_count, 1)
    biases = dt_bias.reshape(head_count, ratio_count, 1)
    decay = -rates * jax.nn.softplus(decay_part.astype(jnp.float32) + biases)
    strength = jax.nn.sigmoid(beta_part.astype(jnp.float32)).reshape(head_count, ratio_count, blocks_total, SPAN)
    cumulative = jnp.cumsum(decay.reshape(head_count, ratio_count, blocks_total, SPAN), axis=-1)
    later = jnp.arange(SPAN)[:, None] > jnp.arange(SPAN)[None, :]
    seen = jnp.arange(SPAN)[:, None] >= jnp.arange(SPAN)[None, :]
    spread = cumulative[..., :, None] - cumulative[..., None, :]
    gram = product('hdni,hdnj->hnij', keys_norm, keys_norm)
    mixing = jnp.where(later, strength[..., :, None] * gram[:, None] * jnp.exp(jnp.where(later, spread, 0.0)), 0.0)
    solved_system = unit_inverse(mixing).astype(jnp.bfloat16)
    lift = (strength * jnp.exp(cumulative))[:, :, None]
    scaled_keys = (lift * keys_norm[:, None].astype(jnp.float32)).astype(jnp.bfloat16)
    scaled_values = (strength[:, :, None] * values_in.astype(jnp.float32)).astype(jnp.bfloat16)
    weighted_keys = product('hrnij,hrdnj->nhrid', solved_system, scaled_keys).astype(jnp.bfloat16)
    weighted_values = product('hrnij,hrenj->nhrie', solved_system, scaled_values).astype(jnp.bfloat16)
    closing = cumulative[..., -1]
    faded = (jnp.exp(closing[..., None] - cumulative)[:, :, None] * keys_norm[:, None].astype(jnp.float32)).astype(jnp.bfloat16)
    faded = jnp.moveaxis(faded, 3, 0)
    keeping = jnp.moveaxis(jnp.exp(closing), 2, 0)

    def advance(carry, pieces):
        keys_step, step_values, faded_step, keep_step, fresh = pieces
        current = jnp.where(fresh, 0.0, carry)
        entering = current.astype(jnp.bfloat16)
        new_values = (step_values.astype(jnp.float32) - product('hrid,hrde->hrie', keys_step, entering)).astype(jnp.bfloat16)
        leaving = keep_step[:, :, None, None] * current + product('hrdi,hrie->hrde', faded_step, new_values)
        return (leaving, (leaving, new_values))
    start_state = jnp.zeros((head_count, ratio_count, DK, DV), jnp.float32)
    unused, (leaving_all, new_all) = lax.scan(advance, start_state, (weighted_keys, weighted_values, faded, keeping, first_block))
    previous = jnp.concatenate([start_state[None], leaving_all[:-1]], axis=0)
    entering_all = jnp.where(first_block[:, None, None, None, None], 0.0, previous).astype(jnp.bfloat16)
    scores = jnp.where(seen, product('hdni,hdnj->hnij', queries, keys_norm)[:, None] * jnp.exp(jnp.where(seen, spread, 0.0)), 0.0).astype(jnp.bfloat16)
    core_out = jnp.exp(cumulative)[:, :, None] * product('hdni,nhrde->hreni', queries, entering_all) + product('hrnij,nhrje->hreni', scores, new_all)
    core_out = core_out.astype(jnp.bfloat16).reshape(head_count, ratio_count * DV, length)
    return (core_out, leaving_all)

def gated_norm(core_out, gate, gain):
    shape_in = core_out.shape
    split_shape = shape_in[:-2] + (shape_in[-2] // DV, DV, shape_in[-1])
    values_wide = core_out.astype(jnp.float32).reshape(split_shape)
    inverse_rms = lax.rsqrt(lax.optimization_barrier(jnp.mean(values_wide * values_wide, axis=-2, keepdims=True)) + EPSILON)
    gate_wide = gate.astype(jnp.float32).reshape(split_shape)
    result = values_wide * inverse_rms * gain[:, None] * jax.nn.silu(gate_wide)
    return result.astype(jnp.bfloat16).reshape(shape_in)

def request_tails(pre_conv, end_tokens):
    positions = (end_tokens[:, None] - (KERNEL - 1) + jnp.arange(KERNEL - 1, dtype=jnp.int32)[None, :]).reshape(-1)
    picked = jnp.take(pre_conv, positions, axis=2)
    picked = picked.reshape(pre_conv.shape[0], pre_conv.shape[1], -1, KERNEL - 1)
    return jnp.transpose(picked, (2, 3, 0, 1))

def reference(mixed, decay_in, beta_in, gate_z, conv_weight, a_log, dt_bias, norm_gain, req_blocks, replica_of, finished):

    def one_pack(pieces):
        pre_conv, decay_part, beta_part, gate_part, blocks = pieces
        begins, end_tokens, first_block, last_block = request_bounds(blocks, pre_conv.shape[-1])
        convolved = causal_conv(pre_conv, conv_weight, begins)
        core_out, leaving_all = delta_heads(convolved, decay_part, beta_part, a_log, dt_bias, first_block)
        normed = gated_norm(core_out, gate_part, norm_gain)
        finals = jnp.take(leaving_all, last_block, axis=0)
        tail_rows = request_tails(pre_conv, end_tokens)
        return (normed, finals, tail_rows)
    mixer_out, finals, tail_rows = lax.map(one_pack, (mixed, decay_in, beta_in, gate_z, req_blocks))
    flat_dest = replica_of.reshape(-1)
    flat_done = finished.reshape(-1)
    member = ((flat_dest[:, None] == jnp.arange(N_REP, dtype=jnp.int32)[None, :]) & (flat_done[:, None] > 0)).astype(jnp.int32)
    order_rank = jnp.cumsum(member, axis=0).astype(jnp.int32) - member
    chosen = ((member[None] > 0) & (order_rank[None] == jnp.arange(SLOTS, dtype=jnp.int32)[:, None, None])).astype(jnp.float32)
    state_rows = finals.reshape(N_REP * REQS, HV, DK, DV)
    tail_flat = tail_rows.reshape(N_REP * REQS, KERNEL - 1, HK, GROUP_CH).astype(jnp.float32)
    states_out = jnp.einsum('sqd,qhab->dshab', chosen, state_rows, precision=lax.Precision.HIGHEST)
    tails_out = jnp.einsum('sqd,qkhc->dskhc', chosen, tail_flat, precision=lax.Precision.HIGHEST).astype(jnp.bfloat16)
    return (mixer_out, states_out, tails_out)
```

```python
import jax
import jax.numpy as jnp
from jax import lax
from jax.experimental import pallas as pl
from jax.experimental.pallas import tpu as pltpu
from jax.sharding import PartitionSpec as P

f32, bf16 = jnp.float32, jnp.bfloat16
NC, T, SPAN = 16, 128, 64

def dot(a, b):
    return jnp.dot(a, b, preferred_element_type=f32)

def dot_nt(a, b):
    return lax.dot_general(a, b, (((1,), (1,)), ((), ())), preferred_element_type=f32)

def iota(shape, d):
    return lax.broadcasted_iota(jnp.int32, shape, d)

def setup_tables(s):
    j, i = iota((T, T), 0), iota((T, T), 1)
    same = (j // SPAN) == (i // SPAN)
    s.seen[...] = jnp.where(same & (j <= i), 1.0, 0.0)
    s.later[...] = jnp.where(same & (j < i), 1.0, 0.0)
    s.eye[...] = jnp.where(j == i, 1.0, 0.0)
    for level in range(6):
        s.level[level] = jnp.where(((j ^ i) >> level) == 1, 1.0, 0.0).astype(bf16)
    taps = s.conv_weight[...].reshape(4, 512).astype(f32)
    taps = jnp.concatenate([taps, jnp.zeros((4, 512), f32)], axis=0).T
    for tap in range(4):
        s.taps[tap] = jnp.broadcast_to(taps[:, tap:tap + 1], (512, T))
    block = iota((32, T), 0)
    start = jnp.int32(0)
    hit = jnp.zeros((32, T), f32)
    for q in range(8):
        hit = jnp.where(block == start, 1.0, hit)
        start = start + s.req_blocks[0, q]
    s.stay[...] = 1.0 - hit

def setup_gates(s):
    lane = iota((NC, T), 1)
    for r in range(2):
        x = s.aux[:, r, :] + s.dt_bias[r]
        rate = jnp.exp(jnp.full((NC, T), s.a_log[r], f32))
        decay = -rate * (jnp.maximum(x, 0.0) + jnp.log1p(jnp.exp(-jnp.abs(x))))
        c = decay
        for sh in (1, 2, 4, 8, 16, 32):
            c = c + jnp.where(lane % SPAN >= sh, pltpu.roll(c, sh, 1), 0.0)
        end0 = jnp.broadcast_to(c[:, SPAN - 1:SPAN], (NC, T))
        end1 = jnp.broadcast_to(c[:, T - 1:T], (NC, T))
        s.cum[r] = c
        s.fade[r] = jnp.exp(jnp.where(lane < SPAN, end0, end1) - c)
        s.lift[r] = jnp.exp(c)
        s.beta[r] = 1.0 / (1.0 + jnp.exp(-s.aux[:, 2 + r, :]))
        s.keep[r, 0] = jnp.exp(end0)
        s.keep[r, 1] = jnp.exp(end1)

def row(ref, c):
    return ref[pl.ds(c, 1), :]

def prep_chunk(s, c):
    before = lax.rem(c + NC - 1, NC)
    lane = iota((1, T), 1)
    token = lane + c * T
    start = jnp.int32(0)
    since = token
    for q in range(7):
        start = start + s.req_blocks[0, q] * SPAN
        since = jnp.where(token >= start, token - start, since)
    now = s.x[c]
    old = s.x[before]
    parts = []
    for g in range(4):
        rows = slice(g * T, (g + 1) * T)
        cur = now[rows].astype(f32)
        prev = old[rows].astype(f32)
        total = s.taps[3, rows, :] * cur
        for back in (1, 2, 3):
            moved = pltpu.roll(jnp.where(lane >= T - back, prev, cur), back, 1)
            total = total + s.taps[3 - back, rows, :] * jnp.where(since >= back, moved, 0.0)
        parts.append(total / (1.0 + jnp.exp(-total)))
    qT = parts[0].astype(bf16)
    kw = parts[1].astype(bf16).astype(f32)
    kT32 = kw * lax.rsqrt(jnp.sum(kw * kw, axis=0, keepdims=True) + 1e-6)
    kT = kT32.astype(bf16)
    kT32 = kT.astype(f32)
    k = kT32.T.astype(bf16)
    both = dot(k, jnp.concatenate([kT, qT], axis=1))
    gram, raw = both[:, :T], both[:, T:]
    zero = jnp.zeros((SPAN, T), bf16)
    kk = jnp.concatenate([
        jnp.concatenate([k[:SPAN], zero], axis=0),
        jnp.concatenate([zero, k[SPAN:]], axis=0)], axis=1)
    seen, later = s.seen[...], s.later[...]
    minus, scaled = [], []
    for r in range(2):
        cum = row(s.cum.at[r], c)
        col = jnp.broadcast_to(cum, (T, T)).T
        e = jnp.exp((cum - col) * seen) * seen
        s.score[c, r] = (raw * e).astype(bf16)
        n = gram * e * later * row(s.beta.at[r], c)
        minus.append(n)
    low = [n.astype(bf16) for n in minus]
    u = [(s.eye[...] - n * s.level[0].astype(f32)).astype(bf16) for n in minus]
    for level in range(1, 6):
        p = [dot(u[r], low[r] * s.level[level]).astype(bf16) for r in range(2)]
        u = [u[r] - dot(p[r], u[r]).astype(bf16) for r in range(2)]
    for r in range(2):
        rest = (minus[r] - low[r].astype(f32)).astype(bf16)
        nx = dot(jnp.concatenate([low[r], rest], axis=0), u[r])
        res = s.eye[...] - u[r].astype(f32) - (nx[:T] + nx[T:])
        u[r] = (u[r].astype(f32) + dot(u[r], res.astype(bf16))).astype(bf16)
    for r in range(2):
        beta = row(s.beta.at[r], c)
        sk = (kT32 * (beta * row(s.lift.at[r], c))).astype(bf16)
        sv = (parts[2 + r].astype(bf16).astype(f32) * beta).astype(bf16)
        w = dot(jnp.concatenate([sv, sk], axis=0), u[r])
        wb = w.astype(bf16)
        s.wv[c, r] = wb[:T]
        s.wq[c, r, :, :T] = wb[T:]
        s.wq[c, r, :, T:] = qT
        gw = dot((w * row(s.fade.at[r], c)).astype(bf16), kk)
        for b in range(2):
            s.add[c, r, b] = gw[:T, b * T:(b + 1) * T]
            s.turn[c, r, b] = gw[T:, b * T:(b + 1) * T].astype(bf16)
    j, i = iota((16, T), 0), iota((16, T), 1)
    pick = jnp.where((j % 8 < 3) & (i == (j // 8) * SPAN + SPAN - 3 + j % 8), 1.0, 0.0).astype(bf16)
    tails = dot_nt(pick, now)
    s.tails[2 * c] = tails[:8]
    s.tails[2 * c + 1] = tails[8:]

def scan_blocks(s):
    def step(c, carry):
        state = list(carry)
        for b in range(2):
            stay = row(s.stay, 2 * c + b)
            for r in range(2):
                inside = state[r] * stay
                low = inside.astype(bf16)
                s.enter[c, r, b * T:(b + 1) * T, :] = low
                state[r] = (row(s.keep.at[r, b], c) * inside + s.add[c, r, b]) - dot(low, s.turn[c, r, b])
                s.leave[2 * c + b, r] = state[r].astype(bf16)
        return tuple(state)
    zero = jnp.zeros((T, T), f32)
    lax.fori_loop(0, NC, step, (zero, zero))

def post_chunk(s, c):
    lane = iota((1, T), 1)
    for r in range(2):
        both = dot(s.enter[c, r], s.wq[c, r])
        first = lane < SPAN
        seenk = jnp.where(first, both[:T, :T], both[T:, :T])
        seenq = jnp.where(first, both[:T, T:], both[T:, T:])
        new = (s.wv[c, r].astype(f32) - seenk).astype(bf16)
        out = row(s.lift.at[r], c) * seenq + dot(new, s.score[c, r])
        s.core[c, r * T:(r + 1) * T, :] = out.astype(bf16)

SCRATCH = dict(
    x=((NC, 512, T), bf16), aux=((NC, 8, T), f32),
    cum=((2, NC, T), f32), fade=((2, NC, T), f32), lift=((2, NC, T), f32), beta=((2, NC, T), f32),
    keep=((2, 2, NC, T), f32), stay=((32, T), f32),
    seen=((T, T), f32), later=((T, T), f32), eye=((T, T), f32), level=((6, T, T), bf16),
    taps=((4, 512, T), f32),
    wv=((NC, 2, T, T), bf16), wq=((NC, 2, T, 2 * T), bf16), score=((NC, 2, T, T), bf16),
    add=((NC, 2, 2, T, T), f32), turn=((NC, 2, 2, T, T), bf16),
    enter=((NC, 2, 2 * T, T), bf16), leave=((32, 2, T, T), bf16),
    core=((NC, 256, T), bf16), tails=((32, 8, 512), f32),
)

class Refs:
    pass


N_SEQ, N_REP, REQS, CAP = 16, 8, 8, 2
MESH = pl.DeviceIdType.MESH
VMEM = pl.BlockSpec(memory_space=pltpu.VMEM)
SMEM = pl.BlockSpec(memory_space=pltpu.SMEM)
ANY = pl.BlockSpec(memory_space=pl.ANY)
SCRATCH_NAMES = list(SCRATCH)


def fill_slots(s):
    keys, lasts = [], []
    last = jnp.int32(-1)
    for q in range(REQS):
        last = last + s.req_blocks[0, q]
        rank = jnp.int32(0)
        for p in range(q):
            hit = (s.replica_of[0, p] == s.replica_of[0, q]) & (s.finished[0, p] > 0)
            rank = rank + jnp.where(hit, 1, 0)
        keys.append(jnp.where(s.finished[0, q] > 0, s.replica_of[0, q] * CAP + rank, -1))
        lasts.append(last)
    for m in range(N_REP * CAP):
        where, used = jnp.int32(0), jnp.int32(0)
        for q in range(REQS):
            where = where + jnp.where(keys[q] == m, lasts[q], 0)
            used = used + jnp.where(keys[q] == m, 1, 0)
        s.slot_block[m] = where
        s.slot_used[m] = used


def build_slot(s, d, k):
    m = d * CAP + k
    block, used = s.slot_block[m], s.slot_used[m].astype(f32)
    for r in range(2):
        flipped = dot_nt(s.eye[...].astype(bf16), s.leave[block, r])
        s.out_states[d, k, r] = (flipped * used).astype(bf16)
    count = (s.slot_used[d * CAP] + s.slot_used[d * CAP + 1]).astype(f32)
    rows = s.tails[block] * used
    return jnp.where(iota((8, 512), 0) == 3, count, rows)


def main_kernel(mixed, decay_in, beta_in, conv_weight, a_log, dt_bias, req_blocks, replica_of, finished,
                back, got_states, got_tails, *scratch):
    s = Refs()
    names = SCRATCH_NAMES + [
        "aux_out", "out_states", "out_tails", "slot_block", "slot_used",
        "x_send", "x_recv", "aux_send", "aux_recv", "core_send", "core_recv",
        "st_send", "st_recv", "tl_send", "tl_recv", "own"]
    for name, ref in zip(names, scratch):
        setattr(s, name, ref)
    s.conv_weight, s.a_log, s.dt_bias, s.req_blocks = conv_weight, a_log, dt_bias, req_blocks
    s.replica_of, s.finished = replica_of, finished
    me, rep = lax.axis_index("seq"), lax.axis_index("rep")

    barrier = pltpu.get_barrier_semaphore()
    for k in range(1, N_SEQ):
        pl.semaphore_signal(barrier, inc=1, device_id={"seq": lax.rem(me + k, N_SEQ)}, device_id_type=MESH)
    for k in range(1, N_REP):
        pl.semaphore_signal(barrier, inc=1, device_id={"rep": lax.rem(rep + k, N_REP)}, device_id_type=MESH)
    for h in range(N_SEQ):
        s.aux_out[h, 0:2, :] = decay_in[0, h].astype(f32)
        s.aux_out[h, 2:4, :] = beta_in[0, h].astype(f32)
        s.aux_out[h, 4:8, :] = jnp.zeros((4, T), f32)

    own_x = pltpu.make_async_copy(mixed.at[0, me], s.x.at[me], s.own.at[0])
    own_aux = pltpu.make_async_copy(s.aux_out.at[me], s.aux.at[me], s.own.at[1])
    own_x.start()
    own_aux.start()
    pl.semaphore_wait(barrier, N_SEQ + N_REP - 2)

    def aux_copy(k):
        to = lax.rem(me + N_SEQ - k, N_SEQ)
        return pltpu.make_async_remote_copy(
            src_ref=s.aux_out.at[to], dst_ref=s.aux.at[me], send_sem=s.aux_send.at[k], recv_sem=s.aux_recv.at[k],
            device_id={"seq": to}, device_id_type=MESH)

    def x_copy(k):
        to = lax.rem(me + N_SEQ - k, N_SEQ)
        return pltpu.make_async_remote_copy(
            src_ref=mixed.at[0, to], dst_ref=s.x.at[me], send_sem=s.x_send.at[k], recv_sem=s.x_recv.at[k],
            device_id={"seq": to}, device_id_type=MESH)

    def start_inputs(k, carry):
        aux_copy(k).start()
        x_copy(k).start()
        return carry

    lax.fori_loop(1, N_SEQ, start_inputs, 0)
    setup_tables(s)
    fill_slots(s)
    own_x.wait()
    own_aux.wait()

    def wait_aux(k, carry):
        aux_copy(k).wait_recv()
        return carry

    lax.fori_loop(1, N_SEQ, wait_aux, 0)
    setup_gates(s)

    def prep(k, carry):
        @pl.when(k < N_SEQ)
        def _():
            x_copy(k).wait_recv()

        prep_chunk(s, lax.rem(me + k, N_SEQ))
        return carry

    lax.fori_loop(1, N_SEQ + 1, prep, 0)
    scan_blocks(s)

    def core_copy(k):
        to = lax.rem(me + k, N_SEQ)
        return pltpu.make_async_remote_copy(
            src_ref=s.core.at[to], dst_ref=back.at[me], send_sem=s.core_send.at[k], recv_sem=s.core_recv.at[k],
            device_id={"seq": to}, device_id_type=MESH)

    def state_copies(k):
        to = lax.rem(rep + k, N_REP)
        return [
            pltpu.make_async_remote_copy(
                src_ref=s.out_states.at[to], dst_ref=got_states.at[rep], send_sem=s.st_send.at[k],
                recv_sem=s.st_recv.at[k], device_id={"rep": to}, device_id_type=MESH),
            pltpu.make_async_remote_copy(
                src_ref=s.out_tails.at[to], dst_ref=got_tails.at[rep], send_sem=s.tl_send.at[k],
                recv_sem=s.tl_recv.at[k], device_id={"rep": to}, device_id_type=MESH)]

    def post(k, carry):
        for half in range(2):
            j = 2 * k - 1 + half
            post_chunk(s, lax.rem(me + j, N_SEQ))

            @pl.when(j < N_SEQ)
            def _():
                core_copy(j).start()

        d = lax.rem(rep + k, N_REP)
        tails = [build_slot(s, d, slot) for slot in range(CAP)]
        s.out_tails[d] = jnp.concatenate(tails, axis=0).astype(bf16)

        @pl.when(k < N_REP)
        def _():
            for copy in state_copies(k):
                copy.start()

        return carry

    lax.fori_loop(1, N_REP + 1, post, 0)
    own = [
        pltpu.make_async_copy(s.core.at[me], back.at[me], s.own.at[2]),
        pltpu.make_async_copy(s.out_states.at[rep], got_states.at[rep], s.own.at[3]),
        pltpu.make_async_copy(s.out_tails.at[rep], got_tails.at[rep], s.own.at[4])]
    for copy in own:
        copy.start()

    def finish_seq(k, carry):
        aux_copy(k).wait_send()
        x_copy(k).wait_send()
        core_copy(k).wait()
        return carry

    def finish_rep(k, carry):
        for copy in state_copies(k):
            copy.wait()
        return carry

    lax.fori_loop(1, N_SEQ, finish_seq, 0)
    lax.fori_loop(1, N_REP, finish_rep, 0)
    for copy in own:
        copy.wait()


HEADS = 4


def finish_kernel(back, gate, gain, got_states, got_tails, mixer, states, tails):
    step = pl.program_id(0)
    column = jnp.broadcast_to(gain[...], (T, T)).T
    for h in range(HEADS):
        for r in range(2):
            rows = slice(r * T, (r + 1) * T)
            value = back[h, rows, :].astype(f32)
            inverse = lax.rsqrt(jnp.mean(value * value, axis=0, keepdims=True) + 1e-6)
            z = gate[0, h, rows, :].astype(f32)
            mixer[0, h, rows, :] = (value * inverse * column * (z / (1.0 + jnp.exp(-z)))).astype(bf16)
    counts = [jnp.max(got_tails[q, 0:8, 0:T].astype(f32)[3:4]).astype(jnp.int32) for q in range(N_REP)]
    bases, base = [], jnp.int32(0)
    for q in range(N_REP):
        bases.append(base)
        base = base + counts[q]
    for h in range(HEADS):
        slot = step * HEADS + h
        pick, used = jnp.int32(0), jnp.int32(0)
        for q in range(N_REP):
            for k in range(CAP):
                hit = (bases[q] + k == slot) & (counts[q] > k)
                pick = pick + jnp.where(hit, q * CAP + k, 0)
                used = used + jnp.where(hit, 1, 0)
        scale = used.astype(f32)
        source, rank = pick // CAP, pick % CAP
        for r in range(2):
            states[0, h, r] = got_states[source, rank, r].astype(f32) * scale
        both = got_tails[source].astype(f32)
        rows = jnp.where(rank == 0, both[0:8], both[8:16]) * scale
        tails[0, h, :, 0, :] = rows[0:3].astype(bf16)


def body(mixed, decay_in, beta_in, gate_z, conv_weight, a_log, dt_bias, norm_gain, req_blocks, replica_of, finished):
    dma = pltpu.SemaphoreType.DMA
    back, got_states, got_tails = pl.pallas_call(
        main_kernel,
        name="main",
        out_shape=[
            jax.ShapeDtypeStruct((N_SEQ, 2 * T, T), bf16),
            jax.ShapeDtypeStruct((N_REP, CAP, 2, T, T), bf16),
            jax.ShapeDtypeStruct((N_REP, 16, 512), bf16)],
        in_specs=[ANY, VMEM, VMEM, VMEM] + [SMEM] * 5,
        out_specs=[ANY] * 3,
        scratch_shapes=[pltpu.VMEM(*SCRATCH[name]) for name in SCRATCH_NAMES] + [
            pltpu.VMEM((N_SEQ, 8, T), f32),
            pltpu.VMEM((N_REP, CAP, 2, T, T), bf16),
            pltpu.VMEM((N_REP, 16, 512), bf16),
            pltpu.SMEM((N_REP * CAP,), jnp.int32),
            pltpu.SMEM((N_REP * CAP,), jnp.int32)] + [dma((N_SEQ,))] * 6 + [dma((N_REP,))] * 4 + [dma((5,))],
        compiler_params=pltpu.CompilerParams(
            collective_id=0, has_side_effects=True, vmem_limit_bytes=48 << 20),
    )(mixed, decay_in, beta_in, conv_weight, a_log, dt_bias, req_blocks, replica_of, finished)
    whole = lambda shape: pl.BlockSpec(shape, lambda i: (0,) * len(shape))
    mixer, states, tails = pl.pallas_call(
        finish_kernel,
        name="finish",
        grid=(N_SEQ // HEADS,),
        out_shape=[
            jax.ShapeDtypeStruct((1, N_SEQ, 2 * T, T), bf16),
            jax.ShapeDtypeStruct((1, N_REP * CAP, 2, T, T), f32),
            jax.ShapeDtypeStruct((1, N_REP * CAP, 3, 1, 512), bf16)],
        in_specs=[
            pl.BlockSpec((HEADS, 2 * T, T), lambda i: (i, 0, 0)),
            pl.BlockSpec((1, HEADS, 2 * T, T), lambda i: (0, i, 0, 0)),
            whole((1, T)),
            whole((N_REP, CAP, 2, T, T)),
            whole((N_REP, 16, 512))],
        out_specs=[
            pl.BlockSpec((1, HEADS, 2 * T, T), lambda i: (0, i, 0, 0)),
            pl.BlockSpec((1, HEADS, 2, T, T), lambda i: (0, i, 0, 0, 0)),
            pl.BlockSpec((1, HEADS, 3, 1, 512), lambda i: (0, i, 0, 0, 0))],
    )(back, gate_z, norm_gain.reshape(1, T), got_states, got_tails)
    return mixer, states, tails


def solution(mesh):
    placed = P("rep", None, None, "seq")
    return jax.shard_map(
        body,
        mesh=mesh,
        in_specs=(placed, placed, placed, placed, P(None, "seq", None), P("seq"), P("seq"), P(),
                  P("rep", None), P("rep", None), P("rep", None)),
        out_specs=(placed, P("rep", None, "seq", None, None), P("rep", None, None, "seq", None)),
        check_vma=False,
    )
```

```python
import jax
import jax.numpy as jnp
from jax import lax
from jax.experimental import pallas as pl
from jax.experimental.pallas import tpu as pltpu
from jax.sharding import PartitionSpec as P

f32, bf16 = jnp.float32, jnp.bfloat16
NC, T, SPAN = 16, 128, 64

def dot(a, b):
    return jnp.dot(a, b, preferred_element_type=f32)

def dot_nt(a, b):
    return lax.dot_general(a, b, (((1,), (1,)), ((), ())), preferred_element_type=f32)

def iota(shape, d):
    return lax.broadcasted_iota(jnp.int32, shape, d)

def setup_tables(s):
    j, i = iota((T, T), 0), iota((T, T), 1)
    same = (j // SPAN) == (i // SPAN)
    s.seen[...] = jnp.where(same & (j <= i), 1.0, 0.0)
    s.later[...] = jnp.where(same & (j < i), 1.0, 0.0)
    s.eye[...] = jnp.where(j == i, 1.0, 0.0)
    for level in range(6):
        s.level[level] = jnp.where(((j ^ i) >> level) == 1, 1.0, 0.0).astype(bf16)
    taps = s.conv_weight[...].reshape(4, 512).astype(f32)
    taps = jnp.concatenate([taps, jnp.zeros((4, 512), f32)], axis=0).T
    for tap in range(4):
        s.taps[tap] = jnp.broadcast_to(taps[:, tap:tap + 1], (512, T))
    block = iota((32, T), 0)
    start = jnp.int32(0)
    hit = jnp.zeros((32, T), f32)
    for q in range(8):
        hit = jnp.where(block == start, 1.0, hit)
        start = start + s.req_blocks[0, q]
    s.stay[...] = 1.0 - hit

def setup_gates(s):
    lane = iota((NC, T), 1)
    for r in range(2):
        x = s.aux[:, r, :] + s.dt_bias[r]
        rate = jnp.exp(jnp.full((NC, T), s.a_log[r], f32))
        decay = -rate * (jnp.maximum(x, 0.0) + jnp.log1p(jnp.exp(-jnp.abs(x))))
        c = decay
        for sh in (1, 2, 4, 8, 16, 32):
            c = c + jnp.where(lane % SPAN >= sh, pltpu.roll(c, sh, 1), 0.0)
        end0 = jnp.broadcast_to(c[:, SPAN - 1:SPAN], (NC, T))
        end1 = jnp.broadcast_to(c[:, T - 1:T], (NC, T))
        s.cum[r] = c
        s.fade[r] = jnp.exp(jnp.where(lane < SPAN, end0, end1) - c)
        s.lift[r] = jnp.exp(c)
        s.beta[r] = 1.0 / (1.0 + jnp.exp(-s.aux[:, 2 + r, :]))
        s.keep[r, 0] = jnp.exp(end0)
        s.keep[r, 1] = jnp.exp(end1)

def row(ref, c):
    return ref[pl.ds(c, 1), :]

def read_chunk(s, c):
    before = lax.rem(c + NC - 1, NC)
    lane = iota((1, T), 1)
    token = lane + c * T
    start = jnp.int32(0)
    since = token
    for q in range(7):
        start = start + s.req_blocks[0, q] * SPAN
        since = jnp.where(token >= start, token - start, since)
    now = s.x[c]
    old = s.x[before]
    parts = []
    for g in range(4):
        rows = slice(g * T, (g + 1) * T)
        cur = now[rows].astype(f32)
        prev = old[rows].astype(f32)
        total = s.taps[3, rows, :] * cur
        for back in (1, 2, 3):
            moved = pltpu.roll(jnp.where(lane >= T - back, prev, cur), back, 1)
            total = total + s.taps[3 - back, rows, :] * jnp.where(since >= back, moved, 0.0)
        parts.append((total / (1.0 + jnp.exp(-total))).astype(bf16))
    qT = parts[0]
    kw = parts[1].astype(f32)
    kT = (kw * lax.rsqrt(jnp.sum(kw * kw, axis=0, keepdims=True) + 1e-6)).astype(bf16)
    k = kT.astype(f32).T.astype(bf16)
    both = dot(k, jnp.concatenate([kT, qT], axis=1))
    gram, raw = both[:, :T], both[:, T:]
    minus = []
    for r in range(2):
        cum = row(s.cum.at[r], c)
        col = jnp.broadcast_to(cum, (T, T)).T
        e = jnp.exp((cum - col) * s.seen[...]) * s.seen[...]
        s.score[c, r] = (raw * e).astype(bf16)
        minus.append(gram * e * (s.later[...] * row(s.beta.at[r], c)))
    j, i = iota((16, T), 0), iota((16, T), 1)
    pick = jnp.where((j % 8 < 3) & (i == (j // 8) * SPAN + SPAN - 3 + j % 8), 1.0, 0.0).astype(bf16)
    tails = dot_nt(pick, now)
    s.tails[2 * c] = tails[:8]
    s.tails[2 * c + 1] = tails[8:]
    return qT, kT, k, parts[2:], minus


def solve(s, minus):
    low = [n.astype(bf16) for n in minus]
    count = range(len(minus))
    u = [(s.eye[...] - n * s.level[0].astype(f32)).astype(bf16) for n in minus]
    for level in range(1, 6):
        p = [dot(u[m], low[m] * s.level[level]).astype(bf16) for m in count]
        u = [u[m] - dot(p[m], u[m]).astype(bf16) for m in count]
    rest = [(minus[m] - low[m].astype(f32)).astype(bf16) for m in count]
    nx = [dot(jnp.concatenate([low[m], rest[m]], axis=0), u[m]) for m in count]
    res = [(s.eye[...] - u[m].astype(f32) - (nx[m][:T] + nx[m][T:])).astype(bf16) for m in count]
    return [(u[m].astype(f32) + dot(u[m], res[m])).astype(bf16) for m in count]


def weigh(s, c, data, u):
    qT, kT, k, values, _ = data
    zero = jnp.zeros((SPAN, T), bf16)
    kk = jnp.concatenate([
        jnp.concatenate([k[:SPAN], zero], axis=0),
        jnp.concatenate([zero, k[SPAN:]], axis=0)], axis=1)
    for r in range(2):
        beta = row(s.beta.at[r], c)
        sk = (kT.astype(f32) * (beta * row(s.lift.at[r], c))).astype(bf16)
        sv = (values[r].astype(f32) * beta).astype(bf16)
        w = dot(jnp.concatenate([sv, sk], axis=0), u[r])
        wb = w.astype(bf16)
        s.wv[c, r] = wb[:T]
        s.wq[c, r, :, :T] = wb[T:]
        s.wq[c, r, :, T:] = qT
        gw = dot((w * row(s.fade.at[r], c)).astype(bf16), kk)
        for b in range(2):
            s.add[c, r, b] = gw[:T, b * T:(b + 1) * T]
            s.turn[c, r, b] = gw[T:, b * T:(b + 1) * T].astype(bf16)


def prep_chunks(s, chunks):
    data = [read_chunk(s, c) for c in chunks]
    minus = [n for d in data for n in d[4]]
    u = solve(s, minus)
    for m, c in enumerate(chunks):
        weigh(s, c, data[m], u[2 * m:2 * m + 2])

def scan_blocks(s):
    def step(c, carry):
        state = list(carry)
        for b in range(2):
            stay = row(s.stay, 2 * c + b)
            for r in range(2):
                inside = state[r] * stay
                low = inside.astype(bf16)
                s.enter[c, r, b * T:(b + 1) * T, :] = low
                state[r] = (row(s.keep.at[r, b], c) * inside + s.add[c, r, b]) - dot(low, s.turn[c, r, b])
                s.leave[2 * c + b, r] = state[r].astype(bf16)
        return tuple(state)
    zero = jnp.zeros((T, T), f32)
    lax.fori_loop(0, NC, step, (zero, zero))

def post_chunks(s, chunks):
    first = iota((1, T), 1) < SPAN
    for c in chunks:
        for r in range(2):
            both = dot(s.enter[c, r], s.wq[c, r])
            seenk = jnp.where(first, both[:T, :T], both[T:, :T])
            seenq = jnp.where(first, both[:T, T:], both[T:, T:])
            new = (s.wv[c, r].astype(f32) - seenk).astype(bf16)
            out = row(s.lift.at[r], c) * seenq + dot(new, s.score[c, r])
            s.core[c, r * T:(r + 1) * T, :] = out.astype(bf16)


SCRATCH = dict(
    x=((NC, 512, T), bf16), aux=((NC, 8, T), f32),
    cum=((2, NC, T), f32), fade=((2, NC, T), f32), lift=((2, NC, T), f32), beta=((2, NC, T), f32),
    keep=((2, 2, NC, T), f32), stay=((32, T), f32),
    seen=((T, T), f32), later=((T, T), f32), eye=((T, T), f32), level=((6, T, T), bf16),
    taps=((4, 512, T), f32),
    wv=((NC, 2, T, T), bf16), wq=((NC, 2, T, 2 * T), bf16), score=((NC, 2, T, T), bf16),
    add=((NC, 2, 2, T, T), f32), turn=((NC, 2, 2, T, T), bf16),
    enter=((NC, 2, 2 * T, T), bf16), leave=((32, 2, T, T), bf16),
    core=((NC, 256, T), bf16), tails=((32, 8, 512), f32),
)

class Refs:
    pass


N_SEQ, N_REP, REQS, CAP = 16, 8, 8, 2
AHEAD = 8
MESH = pl.DeviceIdType.MESH
VMEM = pl.BlockSpec(memory_space=pltpu.VMEM)
SMEM = pl.BlockSpec(memory_space=pltpu.SMEM)
ANY = pl.BlockSpec(memory_space=pl.ANY)
SCRATCH_NAMES = list(SCRATCH)


def fill_slots(s):
    keys, lasts = [], []
    last = jnp.int32(-1)
    for q in range(REQS):
        last = last + s.req_blocks[0, q]
        rank = jnp.int32(0)
        for p in range(q):
            hit = (s.replica_of[0, p] == s.replica_of[0, q]) & (s.finished[0, p] > 0)
            rank = rank + jnp.where(hit, 1, 0)
        keys.append(jnp.where(s.finished[0, q] > 0, s.replica_of[0, q] * CAP + rank, -1))
        lasts.append(last)
    for m in range(N_REP * CAP):
        where, used = jnp.int32(0), jnp.int32(0)
        for q in range(REQS):
            where = where + jnp.where(keys[q] == m, lasts[q], 0)
            used = used + jnp.where(keys[q] == m, 1, 0)
        s.slot_block[m] = where
        s.slot_used[m] = used


def build_slot(s, d, k):
    m = d * CAP + k
    block, used = s.slot_block[m], s.slot_used[m].astype(f32)
    for r in range(2):
        flipped = dot_nt(s.eye[...].astype(bf16), s.leave[block, r])
        s.out_states[d, k, r] = (flipped * used).astype(bf16)
    count = (s.slot_used[d * CAP] + s.slot_used[d * CAP + 1]).astype(f32)
    rows = s.tails[block] * used
    return jnp.where(iota((8, 512), 0) == 3, count, rows)


ORDER = (1, 15, 4, 12, 5, 11, 3, 13, 2, 14, 6, 10, 8, 7, 9)
GROUPS = ((1, 0, 5, 12), (4, 13, 2, 15), (3, 14, 6, 11), (7, 10, 8, 9))
READY = (0, 6, 10, 12, 15)
REP_ORDER = (2, 6, 1, 7, 3, 5, 4, 0)


def entry(table, i):
    out = jnp.int32(table[0])
    for t in range(1, len(table)):
        out = jnp.where(i == t, table[t], out)
    return out


def main_kernel(mixed, decay_in, beta_in, conv_weight, a_log, dt_bias, req_blocks, replica_of, finished,
                back, got_states, got_tails, *scratch):
    s = Refs()
    names = SCRATCH_NAMES + [
        "aux_out", "out_states", "out_tails", "slot_block", "slot_used",
        "x_send", "x_recv", "aux_send", "aux_recv", "core_send", "core_recv",
        "st_send", "st_recv", "tl_send", "tl_recv", "own",
        "decay_in", "beta_in", "conv_weight", "a_log", "dt_bias", "req_blocks", "replica_of", "finished", "small"]
    for name, ref in zip(names, scratch):
        setattr(s, name, ref)
    small = [
        pltpu.make_async_copy(source, target, s.small.at[n]) for n, (source, target) in enumerate((
            (decay_in, s.decay_in), (beta_in, s.beta_in), (conv_weight, s.conv_weight), (a_log, s.a_log),
            (dt_bias, s.dt_bias), (req_blocks, s.req_blocks), (replica_of, s.replica_of), (finished, s.finished)))]
    for copy in small:
        copy.start()
    me, rep = lax.axis_index("seq"), lax.axis_index("rep")

    barrier = pltpu.get_barrier_semaphore()
    for k in range(1, N_SEQ):
        pl.semaphore_signal(barrier, inc=1, device_id={"seq": lax.rem(me + k, N_SEQ)}, device_id_type=MESH)
    for k in range(1, N_REP):
        pl.semaphore_signal(barrier, inc=1, device_id={"rep": lax.rem(rep + k, N_REP)}, device_id_type=MESH)
    for copy in small:
        copy.wait()
    for h in range(N_SEQ):
        s.aux_out[h, 0:2, :] = s.decay_in[0, h].astype(f32)
        s.aux_out[h, 2:4, :] = s.beta_in[0, h].astype(f32)
        s.aux_out[h, 4:8, :] = jnp.zeros((4, T), f32)

    own_x = pltpu.make_async_copy(mixed.at[0, me], s.x.at[me], s.own.at[0])
    own_aux = pltpu.make_async_copy(s.aux_out.at[me], s.aux.at[me], s.own.at[1])
    own_x.start()
    own_aux.start()
    pl.semaphore_wait(barrier, N_SEQ + N_REP - 2)

    def aux_copy(k):
        to = lax.rem(me + N_SEQ - k, N_SEQ)
        return pltpu.make_async_remote_copy(
            src_ref=s.aux_out.at[to], dst_ref=s.aux.at[me], send_sem=s.aux_send.at[k], recv_sem=s.aux_recv.at[k],
            device_id={"seq": to}, device_id_type=MESH)

    def x_copy(k):
        to = lax.rem(me + N_SEQ - k, N_SEQ)
        return pltpu.make_async_remote_copy(
            src_ref=mixed.at[0, to], dst_ref=s.x.at[me], send_sem=s.x_send.at[k], recv_sem=s.x_recv.at[k],
            device_id={"seq": to}, device_id_type=MESH)

    def start_aux(k, carry):
        aux_copy(k).start()
        return carry

    lax.fori_loop(1, N_SEQ, start_aux, 0)
    for n in range(AHEAD):
        x_copy(ORDER[n]).start()
    setup_tables(s)
    fill_slots(s)
    own_x.wait()
    own_aux.wait()

    def wait_aux(k, carry):
        aux_copy(k).wait_recv()
        return carry

    lax.fori_loop(1, N_SEQ, wait_aux, 0)
    setup_gates(s)

    def prep(g, carry):
        for n in range(4):
            @pl.when(g == n)
            def _(n=n):
                for m in range(READY[n], READY[n + 1]):
                    x_copy(ORDER[m]).wait_recv()
                    if m + AHEAD < N_SEQ - 1:
                        x_copy(ORDER[m + AHEAD]).start()

        prep_chunks(s, [lax.rem(me + entry([group[t] for group in GROUPS], g), N_SEQ) for t in range(4)])
        return carry

    lax.fori_loop(0, 4, prep, 0)
    scan_blocks(s)

    def core_copy(k):
        to = lax.rem(me + k, N_SEQ)
        return pltpu.make_async_remote_copy(
            src_ref=s.core.at[to], dst_ref=back.at[me], send_sem=s.core_send.at[k], recv_sem=s.core_recv.at[k],
            device_id={"seq": to}, device_id_type=MESH)

    def state_copies(k):
        to = lax.rem(rep + k, N_REP)
        return [
            pltpu.make_async_remote_copy(
                src_ref=s.out_states.at[to], dst_ref=got_states.at[rep], send_sem=s.st_send.at[k],
                recv_sem=s.st_recv.at[k], device_id={"rep": to}, device_id_type=MESH),
            pltpu.make_async_remote_copy(
                src_ref=s.out_tails.at[to], dst_ref=got_tails.at[rep], send_sem=s.tl_send.at[k],
                recv_sem=s.tl_recv.at[k], device_id={"rep": to}, device_id_type=MESH)]

    def post(g, carry):
        steps = [entry([(ORDER + (0,))[4 * n + t] for n in range(4)], g) for t in range(4)]
        post_chunks(s, [lax.rem(me + k, N_SEQ) for k in steps])
        for t in range(4):
            @pl.when(steps[t] > 0)
            def _(t=t):
                core_copy(steps[t]).start()

        for t in range(2):
            k = entry([REP_ORDER[2 * n + t] for n in range(4)], g)
            d = lax.rem(rep + k, N_REP)
            tails = [build_slot(s, d, slot) for slot in range(CAP)]
            s.out_tails[d] = jnp.concatenate(tails, axis=0).astype(bf16)

            @pl.when(k > 0)
            def _(k=k):
                for copy in state_copies(k):
                    copy.start()

        return carry

    lax.fori_loop(0, 4, post, 0)
    own = [
        pltpu.make_async_copy(s.core.at[me], back.at[me], s.own.at[2]),
        pltpu.make_async_copy(s.out_states.at[rep], got_states.at[rep], s.own.at[3]),
        pltpu.make_async_copy(s.out_tails.at[rep], got_tails.at[rep], s.own.at[4])]
    for copy in own:
        copy.start()

    def finish_seq(k, carry):
        aux_copy(k).wait_send()
        x_copy(k).wait_send()
        core_copy(k).wait()
        return carry

    def finish_rep(k, carry):
        for copy in state_copies(k):
            copy.wait()
        return carry

    lax.fori_loop(1, N_SEQ, finish_seq, 0)
    lax.fori_loop(1, N_REP, finish_rep, 0)
    for copy in own:
        copy.wait()


HEADS = 4


def finish_kernel(back, gate, gain, got_states, got_tails, mixer, states, tails):
    step = pl.program_id(0)
    column = jnp.broadcast_to(gain[...], (T, T)).T
    for h in range(HEADS):
        for r in range(2):
            rows = slice(r * T, (r + 1) * T)
            value = back[h, rows, :].astype(f32)
            inverse = lax.rsqrt(jnp.mean(value * value, axis=0, keepdims=True) + 1e-6)
            z = gate[0, h, rows, :].astype(f32)
            mixer[0, h, rows, :] = (value * inverse * column * (z / (1.0 + jnp.exp(-z)))).astype(bf16)
    counts = [jnp.max(got_tails[q, 0:8, 0:T].astype(f32)[3:4]).astype(jnp.int32) for q in range(N_REP)]
    bases, base = [], jnp.int32(0)
    for q in range(N_REP):
        bases.append(base)
        base = base + counts[q]
    for h in range(HEADS):
        slot = step * HEADS + h
        pick, used = jnp.int32(0), jnp.int32(0)
        for q in range(N_REP):
            for k in range(CAP):
                hit = (bases[q] + k == slot) & (counts[q] > k)
                pick = pick + jnp.where(hit, q * CAP + k, 0)
                used = used + jnp.where(hit, 1, 0)
        scale = used.astype(f32)
        source, rank = pick // CAP, pick % CAP
        for r in range(2):
            states[0, h, r] = got_states[source, rank, r].astype(f32) * scale
        both = got_tails[source].astype(f32)
        rows = jnp.where(rank == 0, both[0:8], both[8:16]) * scale
        tails[0, h, :, 0, :] = rows[0:3].astype(bf16)


def body(mixed, decay_in, beta_in, gate_z, conv_weight, a_log, dt_bias, norm_gain, req_blocks, replica_of, finished):
    dma = pltpu.SemaphoreType.DMA
    back, got_states, got_tails = pl.pallas_call(
        main_kernel,
        name="main",
        out_shape=[
            jax.ShapeDtypeStruct((N_SEQ, 2 * T, T), bf16),
            jax.ShapeDtypeStruct((N_REP, CAP, 2, T, T), bf16),
            jax.ShapeDtypeStruct((N_REP, 16, 512), bf16)],
        in_specs=[ANY] * 9,
        out_specs=[ANY] * 3,
        scratch_shapes=[pltpu.VMEM(*SCRATCH[name]) for name in SCRATCH_NAMES] + [
            pltpu.VMEM((N_SEQ, 8, T), f32),
            pltpu.VMEM((N_REP, CAP, 2, T, T), bf16),
            pltpu.VMEM((N_REP, 16, 512), bf16),
            pltpu.SMEM((N_REP * CAP,), jnp.int32),
            pltpu.SMEM((N_REP * CAP,), jnp.int32)] + [dma((N_SEQ,))] * 6 + [dma((N_REP,))] * 4 + [
                dma((5,)),
                pltpu.VMEM(decay_in.shape, bf16), pltpu.VMEM(beta_in.shape, bf16), pltpu.VMEM(conv_weight.shape, bf16),
                pltpu.SMEM(a_log.shape, f32), pltpu.SMEM(dt_bias.shape, f32), pltpu.SMEM(req_blocks.shape, jnp.int32),
                pltpu.SMEM(replica_of.shape, jnp.int32), pltpu.SMEM(finished.shape, jnp.int32), dma((8,))],
        compiler_params=pltpu.CompilerParams(
            collective_id=0, has_side_effects=True, vmem_limit_bytes=48 << 20),
    )(mixed, decay_in, beta_in, conv_weight, a_log, dt_bias, req_blocks, replica_of, finished)
    whole = lambda shape: pl.BlockSpec(shape, lambda i: (0,) * len(shape))
    mixer, states, tails = pl.pallas_call(
        finish_kernel,
        name="finish",
        grid=(N_SEQ // HEADS,),
        out_shape=[
            jax.ShapeDtypeStruct((1, N_SEQ, 2 * T, T), bf16),
            jax.ShapeDtypeStruct((1, N_REP * CAP, 2, T, T), f32),
            jax.ShapeDtypeStruct((1, N_REP * CAP, 3, 1, 512), bf16)],
        in_specs=[
            pl.BlockSpec((HEADS, 2 * T, T), lambda i: (i, 0, 0)),
            pl.BlockSpec((1, HEADS, 2 * T, T), lambda i: (0, i, 0, 0)),
            whole((1, T)),
            whole((N_REP, CAP, 2, T, T)),
            whole((N_REP, 16, 512))],
        out_specs=[
            pl.BlockSpec((1, HEADS, 2 * T, T), lambda i: (0, i, 0, 0)),
            pl.BlockSpec((1, HEADS, 2, T, T), lambda i: (0, i, 0, 0, 0)),
            pl.BlockSpec((1, HEADS, 3, 1, 512), lambda i: (0, i, 0, 0, 0))],
    )(back, gate_z, norm_gain.reshape(1, T), got_states, got_tails)
    return mixer, states, tails


def solution(mesh):
    placed = P("rep", None, None, "seq")
    return jax.shard_map(
        body,
        mesh=mesh,
        in_specs=(placed, placed, placed, placed, P(None, "seq", None), P("seq"), P("seq"), P(),
                  P("rep", None), P("rep", None), P("rep", None)),
        out_specs=(placed, P("rep", None, "seq", None, None), P("rep", None, None, "seq", None)),
        check_vma=False,
    )
```

```python
import jax
import jax.numpy as jnp
from jax import lax
from jax.experimental import pallas as pl
from jax.experimental.pallas import tpu as pltpu
from jax.sharding import PartitionSpec as P

f32, bf16 = jnp.float32, jnp.bfloat16
NC, T, SPAN = 16, 128, 64

def dot(a, b):
    return jnp.dot(a, b, preferred_element_type=f32)

def dot_nt(a, b):
    return lax.dot_general(a, b, (((1,), (1,)), ((), ())), preferred_element_type=f32)

def iota(shape, d):
    return lax.broadcasted_iota(jnp.int32, shape, d)

def setup_tables(s):
    j, i = iota((T, T), 0), iota((T, T), 1)
    same = (j // SPAN) == (i // SPAN)
    s.seen[...] = jnp.where(same & (j <= i), 1.0, 0.0)
    s.later[...] = jnp.where(same & (j < i), 1.0, 0.0)
    s.eye[...] = jnp.where(j == i, 1.0, 0.0)
    for level in range(6):
        s.level[level] = jnp.where(((j ^ i) >> level) == 1, 1.0, 0.0).astype(bf16)
    taps = s.conv_weight[...].reshape(4, 512).astype(f32)
    taps = jnp.concatenate([taps, jnp.zeros((4, 512), f32)], axis=0).T
    for tap in range(4):
        s.taps[tap] = jnp.broadcast_to(taps[:, tap:tap + 1], (512, T))
    block = iota((32, T), 0)
    start = jnp.int32(0)
    hit = jnp.zeros((32, T), f32)
    for q in range(8):
        hit = jnp.where(block == start, 1.0, hit)
        start = start + s.req_blocks[0, q]
    s.stay[...] = 1.0 - hit

def setup_gates(s):
    lane = iota((NC, T), 1)
    for r in range(2):
        x = s.aux[:, r, :] + s.dt_bias[r]
        rate = jnp.exp(jnp.full((NC, T), s.a_log[r], f32))
        decay = -rate * (jnp.maximum(x, 0.0) + jnp.log1p(jnp.exp(-jnp.abs(x))))
        c = decay
        for sh in (1, 2, 4, 8, 16, 32):
            c = c + jnp.where(lane % SPAN >= sh, pltpu.roll(c, sh, 1), 0.0)
        end0 = jnp.broadcast_to(c[:, SPAN - 1:SPAN], (NC, T))
        end1 = jnp.broadcast_to(c[:, T - 1:T], (NC, T))
        s.cum[r] = c
        s.fade[r] = jnp.exp(jnp.where(lane < SPAN, end0, end1) - c)
        s.lift[r] = jnp.exp(c)
        s.beta[r] = 1.0 / (1.0 + jnp.exp(-s.aux[:, 2 + r, :]))
        s.keep[r, 0] = jnp.exp(end0)
        s.keep[r, 1] = jnp.exp(end1)

def row(ref, c):
    return ref[pl.ds(c, 1), :]

def read_chunk(s, c):
    before = lax.rem(c + NC - 1, NC)
    lane = iota((1, T), 1)
    token = lane + c * T
    start = jnp.int32(0)
    since = token
    for q in range(7):
        start = start + s.req_blocks[0, q] * SPAN
        since = jnp.where(token >= start, token - start, since)
    now = s.x[c]
    old = s.x[before]
    parts = []
    for g in range(4):
        rows = slice(g * T, (g + 1) * T)
        cur = now[rows].astype(f32)
        prev = old[rows].astype(f32)
        total = s.taps[3, rows, :] * cur
        for back in (1, 2, 3):
            moved = pltpu.roll(jnp.where(lane >= T - back, prev, cur), back, 1)
            total = total + s.taps[3 - back, rows, :] * jnp.where(since >= back, moved, 0.0)
        parts.append((total / (1.0 + jnp.exp(-total))).astype(bf16))
    qT = parts[0]
    kw = parts[1].astype(f32)
    kT = (kw * lax.rsqrt(jnp.sum(kw * kw, axis=0, keepdims=True) + 1e-6)).astype(bf16)
    k = kT.astype(f32).T.astype(bf16)
    both = dot(k, jnp.concatenate([kT, qT], axis=1))
    gram, raw = both[:, :T], both[:, T:]
    minus = []
    for r in range(2):
        cum = row(s.cum.at[r], c)
        col = jnp.broadcast_to(cum, (T, T)).T
        e = jnp.exp((cum - col) * s.seen[...]) * s.seen[...]
        s.score[c, r] = (raw * e).astype(bf16)
        minus.append(gram * e * (s.later[...] * row(s.beta.at[r], c)))
    j, i = iota((16, T), 0), iota((16, T), 1)
    pick = jnp.where((j % 8 < 3) & (i == (j // 8) * SPAN + SPAN - 3 + j % 8), 1.0, 0.0).astype(bf16)
    tails = dot_nt(pick, now)
    s.tails[2 * c] = tails[:8]
    s.tails[2 * c + 1] = tails[8:]
    return qT, kT, k, parts[2:], minus


def solve(s, minus):
    low = [n.astype(bf16) for n in minus]
    count = range(len(minus))
    u = [(s.eye[...] - n * s.level[0].astype(f32)).astype(bf16) for n in minus]
    for level in range(1, 6):
        p = [dot(u[m], low[m] * s.level[level]).astype(bf16) for m in count]
        u = [u[m] - dot(p[m], u[m]).astype(bf16) for m in count]
    rest = [(minus[m] - low[m].astype(f32)).astype(bf16) for m in count]
    nx = [dot(jnp.concatenate([low[m], rest[m]], axis=0), u[m]) for m in count]
    res = [(s.eye[...] - u[m].astype(f32) - (nx[m][:T] + nx[m][T:])).astype(bf16) for m in count]
    return [(u[m].astype(f32) + dot(u[m], res[m])).astype(bf16) for m in count]


def weigh(s, c, data, u):
    qT, kT, k, values, _ = data
    zero = jnp.zeros((SPAN, T), bf16)
    kk = jnp.concatenate([
        jnp.concatenate([k[:SPAN], zero], axis=0),
        jnp.concatenate([zero, k[SPAN:]], axis=0)], axis=1)
    for r in range(2):
        beta = row(s.beta.at[r], c)
        sk = (kT.astype(f32) * (beta * row(s.lift.at[r], c))).astype(bf16)
        sv = (values[r].astype(f32) * beta).astype(bf16)
        w = dot(jnp.concatenate([sv, sk], axis=0), u[r])
        wb = w.astype(bf16)
        s.wv[c, r] = wb[:T]
        s.wq[c, r, :, :T] = wb[T:]
        s.wq[c, r, :, T:] = qT
        gw = dot((w * row(s.fade.at[r], c)).astype(bf16), kk)
        for b in range(2):
            s.add[c, r, b] = gw[:T, b * T:(b + 1) * T]
            s.turn[c, r, b] = gw[T:, b * T:(b + 1) * T].astype(bf16)


def prep_chunks(s, chunks):
    data = [read_chunk(s, c) for c in chunks]
    minus = [n for d in data for n in d[4]]
    u = solve(s, minus)
    for m, c in enumerate(chunks):
        weigh(s, c, data[m], u[2 * m:2 * m + 2])

def scan_blocks(s):
    def step(c, carry):
        state = list(carry)
        for b in range(2):
            stay = row(s.stay, 2 * c + b)
            for r in range(2):
                inside = state[r] * stay
                low = inside.astype(bf16)
                s.enter[c, r, b * T:(b + 1) * T, :] = low
                state[r] = (row(s.keep.at[r, b], c) * inside + s.add[c, r, b]) - dot(low, s.turn[c, r, b])
                s.leave[2 * c + b, r] = state[r].astype(bf16)
        return tuple(state)
    zero = jnp.zeros((T, T), f32)
    lax.fori_loop(0, NC, step, (zero, zero))

def post_chunks(s, chunks):
    first = iota((1, T), 1) < SPAN
    for c in chunks:
        for r in range(2):
            both = dot(s.enter[c, r], s.wq[c, r])
            seenk = jnp.where(first, both[:T, :T], both[T:, :T])
            seenq = jnp.where(first, both[:T, T:], both[T:, T:])
            new = (s.wv[c, r].astype(f32) - seenk).astype(bf16)
            out = row(s.lift.at[r], c) * seenq + dot(new, s.score[c, r])
            s.core[c, r * T:(r + 1) * T, :] = out.astype(bf16)


SCRATCH = dict(
    x=((NC, 512, T), bf16), aux=((NC, 8, T), f32),
    cum=((2, NC, T), f32), fade=((2, NC, T), f32), lift=((2, NC, T), f32), beta=((2, NC, T), f32),
    keep=((2, 2, NC, T), f32), stay=((32, T), f32),
    seen=((T, T), f32), later=((T, T), f32), eye=((T, T), f32), level=((6, T, T), bf16),
    taps=((4, 512, T), f32),
    wv=((NC, 2, T, T), bf16), wq=((NC, 2, T, 2 * T), bf16), score=((NC, 2, T, T), bf16),
    add=((NC, 2, 2, T, T), f32), turn=((NC, 2, 2, T, T), bf16),
    enter=((NC, 2, 2 * T, T), bf16), leave=((32, 2, T, T), bf16),
    core=((NC, 256, T), bf16), tails=((32, 8, 512), f32),
)

class Refs:
    pass


N_SEQ, N_REP, REQS, CAP = 16, 8, 8, 2
AHEAD = 11
FIRST = False
VMEM_GRANT = 63 << 20
MESH = pl.DeviceIdType.MESH
VMEM = pl.BlockSpec(memory_space=pltpu.VMEM)
SMEM = pl.BlockSpec(memory_space=pltpu.SMEM)
HBM = pl.BlockSpec(memory_space=pltpu.MemorySpace.HBM)
SCRATCH_NAMES = list(SCRATCH)


def fill_slots(s):
    keys, lasts = [], []
    last = jnp.int32(-1)
    for q in range(REQS):
        last = last + s.req_blocks[0, q]
        rank = jnp.int32(0)
        for p in range(q):
            hit = (s.replica_of[0, p] == s.replica_of[0, q]) & (s.finished[0, p] > 0)
            rank = rank + jnp.where(hit, 1, 0)
        keys.append(jnp.where(s.finished[0, q] > 0, s.replica_of[0, q] * CAP + rank, -1))
        lasts.append(last)
    for m in range(N_REP * CAP):
        where, used = jnp.int32(0), jnp.int32(0)
        for q in range(REQS):
            where = where + jnp.where(keys[q] == m, lasts[q], 0)
            used = used + jnp.where(keys[q] == m, 1, 0)
        s.slot_block[m] = where
        s.slot_used[m] = used


def build_slot(s, d, k):
    m = d * CAP + k
    block, used = s.slot_block[m], s.slot_used[m].astype(f32)
    for r in range(2):
        flipped = dot_nt(s.eye[...].astype(bf16), s.leave[block, r])
        s.out_states[d, k, r] = (flipped * used).astype(bf16)
    count = (s.slot_used[d * CAP] + s.slot_used[d * CAP + 1]).astype(f32)
    rows = s.tails[block] * used
    return jnp.where(iota((8, 512), 0) == 3, count, rows)


ORDER = (1, 15, 4, 12, 5, 11, 3, 13, 2, 14, 6, 10, 8, 7, 9)
GROUPS = ((1, 0, 5, 12), (4, 13, 2, 15), (3, 14, 6, 11), (7, 10, 8, 9))
READY = (0, 6, 10, 12, 15)
REP_ORDER = (2, 6, 1, 7, 3, 5, 4, 0)


def entry(table, i):
    out = jnp.int32(table[0])
    for t in range(1, len(table)):
        out = jnp.where(i == t, table[t], out)
    return out


def main_kernel(mixed, decay_in, beta_in, conv_weight, a_log, dt_bias, req_blocks, replica_of, finished,
                back, got_states, got_tails, *scratch):
    s = Refs()
    names = SCRATCH_NAMES + [
        "aux_out", "out_states", "out_tails", "slot_block", "slot_used",
        "x_send", "x_recv", "aux_send", "aux_recv", "core_send", "core_recv",
        "st_send", "st_recv", "tl_send", "tl_recv", "own",
        "decay_in", "beta_in", "conv_weight", "a_log", "dt_bias", "req_blocks", "replica_of", "finished", "small"]
    for name, ref in zip(names, scratch):
        setattr(s, name, ref)
    small = [
        pltpu.make_async_copy(source, target, s.small.at[n]) for n, (source, target) in enumerate((
            (decay_in, s.decay_in), (beta_in, s.beta_in), (conv_weight, s.conv_weight), (a_log, s.a_log),
            (dt_bias, s.dt_bias), (req_blocks, s.req_blocks), (replica_of, s.replica_of), (finished, s.finished)))]
    for copy in small:
        copy.start()
    me, rep = lax.axis_index("seq"), lax.axis_index("rep")

    barrier = pltpu.get_barrier_semaphore()
    for k in range(1, N_SEQ):
        pl.semaphore_signal(barrier, inc=1, device_id={"seq": lax.rem(me + k, N_SEQ)}, device_id_type=MESH)
    for k in range(1, N_REP):
        pl.semaphore_signal(barrier, inc=1, device_id={"rep": lax.rem(rep + k, N_REP)}, device_id_type=MESH)
    for copy in small:
        copy.wait()
    for h in range(N_SEQ):
        s.aux_out[h, 0:2, :] = s.decay_in[0, h].astype(f32)
        s.aux_out[h, 2:4, :] = s.beta_in[0, h].astype(f32)
        s.aux_out[h, 4:8, :] = jnp.zeros((4, T), f32)

    own_x = pltpu.make_async_copy(mixed.at[0, me], s.x.at[me], s.own.at[0])
    own_aux = pltpu.make_async_copy(s.aux_out.at[me], s.aux.at[me], s.own.at[1])
    own_x.start()
    own_aux.start()
    pl.semaphore_wait(barrier, N_SEQ + N_REP - 2)

    def aux_copy(k):
        to = lax.rem(me + N_SEQ - k, N_SEQ)
        return pltpu.make_async_remote_copy(
            src_ref=s.aux_out.at[to], dst_ref=s.aux.at[me], send_sem=s.aux_send.at[k], recv_sem=s.aux_recv.at[k],
            device_id={"seq": to}, device_id_type=MESH)

    def x_copy(k):
        to = lax.rem(me + N_SEQ - k, N_SEQ)
        return pltpu.make_async_remote_copy(
            src_ref=mixed.at[0, to], dst_ref=s.x.at[me], send_sem=s.x_send.at[k], recv_sem=s.x_recv.at[k],
            device_id={"seq": to}, device_id_type=MESH)

    def start_aux(k, carry):
        aux_copy(k).start()
        return carry

    lax.fori_loop(1, N_SEQ, start_aux, 0)
    for n in range(AHEAD):
        x_copy(ORDER[n]).start()
    setup_tables(s)
    fill_slots(s)
    own_x.wait()
    own_aux.wait()

    def wait_aux(k, carry):
        aux_copy(k).wait_recv()
        return carry

    lax.fori_loop(1, N_SEQ, wait_aux, 0)
    setup_gates(s)

    def prep(g, carry):
        for n in range(4):
            @pl.when(g == n)
            def _(n=n):
                for m in range(READY[n], READY[n + 1]):
                    x_copy(ORDER[m]).wait_recv()
                    if m + AHEAD < N_SEQ - 1:
                        x_copy(ORDER[m + AHEAD]).start()

        prep_chunks(s, [lax.rem(me + entry([group[t] for group in GROUPS], g), N_SEQ) for t in range(4)])
        return carry

    lax.fori_loop(0, 4, prep, 0)
    scan_blocks(s)

    def core_copy(k):
        to = lax.rem(me + k, N_SEQ)
        return pltpu.make_async_remote_copy(
            src_ref=s.core.at[to], dst_ref=back.at[me], send_sem=s.core_send.at[k], recv_sem=s.core_recv.at[k],
            device_id={"seq": to}, device_id_type=MESH)

    def state_copies(k):
        to = lax.rem(rep + k, N_REP)
        return [
            pltpu.make_async_remote_copy(
                src_ref=s.out_states.at[to], dst_ref=got_states.at[rep], send_sem=s.st_send.at[k],
                recv_sem=s.st_recv.at[k], device_id={"rep": to}, device_id_type=MESH),
            pltpu.make_async_remote_copy(
                src_ref=s.out_tails.at[to], dst_ref=got_tails.at[rep], send_sem=s.tl_send.at[k],
                recv_sem=s.tl_recv.at[k], device_id={"rep": to}, device_id_type=MESH)]

    def hand_off(g):
        for t in range(2):
            k = entry([REP_ORDER[2 * n + t] for n in range(4)], g)
            d = lax.rem(rep + k, N_REP)
            tails = [build_slot(s, d, slot) for slot in range(CAP)]
            s.out_tails[d] = jnp.concatenate(tails, axis=0).astype(bf16)

            @pl.when(k > 0)
            def _(k=k):
                for copy in state_copies(k):
                    copy.start()

    def post(g, carry):
        steps = [entry([(ORDER + (0,))[4 * n + t] for n in range(4)], g) for t in range(4)]
        post_chunks(s, [lax.rem(me + k, N_SEQ) for k in steps])
        for t in range(4):
            @pl.when(steps[t] > 0)
            def _(t=t):
                core_copy(steps[t]).start()

        if not FIRST:
            hand_off(g)
        return carry

    def hand_off_first(g, carry):
        hand_off(g)
        return carry

    if FIRST:
        lax.fori_loop(0, 4, hand_off_first, 0)
    lax.fori_loop(0, 4, post, 0)
    own = [
        pltpu.make_async_copy(s.core.at[me], back.at[me], s.own.at[2]),
        pltpu.make_async_copy(s.out_states.at[rep], got_states.at[rep], s.own.at[3]),
        pltpu.make_async_copy(s.out_tails.at[rep], got_tails.at[rep], s.own.at[4])]
    for copy in own:
        copy.start()

    def finish_seq(k, carry):
        aux_copy(k).wait_send()
        x_copy(k).wait_send()
        core_copy(k).wait()
        return carry

    def finish_rep(k, carry):
        for copy in state_copies(k):
            copy.wait()
        return carry

    lax.fori_loop(1, N_SEQ, finish_seq, 0)
    lax.fori_loop(1, N_REP, finish_rep, 0)
    for copy in own:
        copy.wait()


def finish_kernel(back_hbm, gate, gain_hbm, got_states_hbm, got_tails_hbm, mixer, states, tails_out,
                  z_in, mixed_out, states_out, back, gain, got_states, got_tails, tails,
                  gate_sem, back_sem, mixer_sem, states_sem, load_sem):
    first = [
        pltpu.make_async_copy(got_tails_hbm, got_tails, load_sem.at[0]),
        pltpu.make_async_copy(got_states_hbm, got_states, load_sem.at[1]),
        pltpu.make_async_copy(gain_hbm, gain, load_sem.at[2])]

    def load(h):
        return [
            pltpu.make_async_copy(gate.at[0, h], z_in.at[h], gate_sem.at[h]),
            pltpu.make_async_copy(back_hbm.at[h], back.at[h], back_sem.at[h])]

    for copy in first:
        copy.start()
    for h in range(N_SEQ):
        for copy in load(h):
            copy.start()
    for copy in first:
        copy.wait()
    counts = [jnp.max(got_tails[q, 0:8, 0:T].astype(f32)[3:4]).astype(jnp.int32) for q in range(N_REP)]
    bases, base = [], jnp.int32(0)
    for q in range(N_REP):
        bases.append(base)
        base = base + counts[q]

    def store_states(slot):
        return pltpu.make_async_copy(states_out.at[slot], states.at[0, slot], states_sem.at[slot])

    def store_mixer(h):
        return pltpu.make_async_copy(mixed_out.at[h], mixer.at[0, h], mixer_sem.at[h])

    def land(slot):
        pick, used = jnp.int32(0), jnp.int32(0)
        for q in range(N_REP):
            rank = slot - bases[q]
            hit = (rank >= 0) & (rank < counts[q])
            pick = jnp.where(hit, q * CAP + rank, pick)
            used = jnp.where(hit, 1, used)
        scale = used.astype(f32)
        source, rank = pick // CAP, pick % CAP
        for r in range(2):
            states_out[slot, r] = got_states[source, rank, r].astype(f32) * scale
        store_states(slot).start()
        both = got_tails[source].astype(f32)
        rows = jnp.where(rank == 0, both[0:8], both[8:16]) * scale
        for p in range(3):
            tails[p, pl.ds(slot, 1), :] = rows[p:p + 1]

    def land_some(g, carry):
        for t in range(4):
            land(g * 4 + t)
        return carry

    lax.fori_loop(0, N_REP * CAP // 4, land_some, 0)
    tails_out[...] = tails[...].astype(bf16)
    column = jnp.broadcast_to(gain[...], (T, T)).T

    def norm(g, carry):
        for t in range(4):
            for copy in load(g * 4 + t):
                copy.wait()
        for t in range(4):
            h = g * 4 + t
            for r in range(2):
                rows = slice(r * T, (r + 1) * T)
                value = back[h, rows, :].astype(f32)
                inverse = lax.rsqrt(jnp.mean(value * value, axis=0, keepdims=True) + 1e-6)
                z = z_in[h, rows, :].astype(f32)
                mixed_out[h, rows, :] = (value * inverse * column * (z / (1.0 + jnp.exp(-z)))).astype(bf16)
        for t in range(4):
            store_mixer(g * 4 + t).start()
        return carry

    lax.fori_loop(0, N_SEQ // 4, norm, 0)

    def drain(h, carry):
        store_states(h).wait()
        store_mixer(h).wait()
        return carry

    lax.fori_loop(0, N_SEQ, drain, 0)


def body(mixed, decay_in, beta_in, gate_z, conv_weight, a_log, dt_bias, norm_gain, req_blocks, replica_of, finished):
    dma = pltpu.SemaphoreType.DMA
    back, got_states, got_tails = pl.pallas_call(
        main_kernel,
        name="main",
        out_shape=[
            jax.ShapeDtypeStruct((N_SEQ, 2 * T, T), bf16),
            jax.ShapeDtypeStruct((N_REP, CAP, 2, T, T), bf16),
            jax.ShapeDtypeStruct((N_REP, 16, 512), bf16)],
        in_specs=[HBM] * 9,
        out_specs=[HBM] * 3,
        scratch_shapes=[pltpu.VMEM(*SCRATCH[name]) for name in SCRATCH_NAMES] + [
            pltpu.VMEM((N_SEQ, 8, T), f32),
            pltpu.VMEM((N_REP, CAP, 2, T, T), bf16),
            pltpu.VMEM((N_REP, 16, 512), bf16),
            pltpu.SMEM((N_REP * CAP,), jnp.int32),
            pltpu.SMEM((N_REP * CAP,), jnp.int32)] + [dma((N_SEQ,))] * 6 + [dma((N_REP,))] * 4 + [
                dma((5,)),
                pltpu.VMEM(decay_in.shape, bf16), pltpu.VMEM(beta_in.shape, bf16), pltpu.VMEM((1, 4, 512), bf16),
                pltpu.SMEM(a_log.shape, f32), pltpu.SMEM(dt_bias.shape, f32), pltpu.SMEM(req_blocks.shape, jnp.int32),
                pltpu.SMEM(replica_of.shape, jnp.int32), pltpu.SMEM(finished.shape, jnp.int32), dma((8,))],
        compiler_params=pltpu.CompilerParams(
            collective_id=0, has_side_effects=True, vmem_limit_bytes=VMEM_GRANT),
    )(mixed, decay_in, beta_in, jnp.transpose(conv_weight, (1, 0, 2)), a_log, dt_bias, req_blocks, replica_of, finished)
    mixer, states, tails = pl.pallas_call(
        finish_kernel,
        name="finish",
        out_shape=[
            jax.ShapeDtypeStruct((1, N_SEQ, 2 * T, T), bf16),
            jax.ShapeDtypeStruct((1, N_REP * CAP, 2, T, T), f32),
            jax.ShapeDtypeStruct((3, N_REP * CAP, 512), bf16)],
        in_specs=[HBM] * 5,
        out_specs=[HBM, HBM, VMEM],
        scratch_shapes=[
            pltpu.VMEM((N_SEQ, 2 * T, T), bf16),
            pltpu.VMEM((N_SEQ, 2 * T, T), bf16),
            pltpu.VMEM((N_REP * CAP, 2, T, T), f32),
            pltpu.VMEM((N_SEQ, 2 * T, T), bf16),
            pltpu.VMEM((1, T), f32),
            pltpu.VMEM((N_REP, CAP, 2, T, T), bf16),
            pltpu.VMEM((N_REP, 16, 512), bf16),
            pltpu.VMEM((3, N_REP * CAP, 512), f32),
            dma((N_SEQ,)), dma((N_SEQ,)), dma((N_SEQ,)), dma((N_REP * CAP,)), dma((3,))],
        compiler_params=pltpu.CompilerParams(vmem_limit_bytes=VMEM_GRANT),
    )(back, gate_z, norm_gain.reshape(1, T), got_states, got_tails)
    tails = jnp.transpose(tails, (1, 0, 2))[None, :, :, None, :]
    return mixer, states, tails


def solution(mesh):
    placed = P("rep", None, None, "seq")
    return jax.shard_map(
        body,
        mesh=mesh,
        in_specs=(placed, placed, placed, placed, P(None, "seq", None), P("seq"), P("seq"), P(),
                  P("rep", None), P("rep", None), P("rep", None)),
        out_specs=(placed, P("rep", None, "seq", None, None), P("rep", None, None, "seq", None)),
        check_vma=False,
    )
```

```python
import jax
import jax.numpy as jnp
from jax import lax
from jax.experimental import pallas as pl
from jax.experimental.pallas import tpu as pltpu
from jax.sharding import PartitionSpec as P

f32, bf16 = jnp.float32, jnp.bfloat16
NC, T, SPAN = 16, 128, 64

def dot(a, b):
    return jnp.dot(a, b, preferred_element_type=f32)

def dot_nt(a, b):
    return lax.dot_general(a, b, (((1,), (1,)), ((), ())), preferred_element_type=f32)

def iota(shape, d):
    return lax.broadcasted_iota(jnp.int32, shape, d)

def setup_tables(s):
    j, i = iota((T, T), 0), iota((T, T), 1)
    same = (j // SPAN) == (i // SPAN)
    s.seen[...] = jnp.where(same & (j <= i), 1.0, 0.0)
    s.later[...] = jnp.where(same & (j < i), 1.0, 0.0)
    s.eye[...] = jnp.where(j == i, 1.0, 0.0)
    for level in range(6):
        s.level[level] = jnp.where(((j ^ i) >> level) == 1, 1.0, 0.0).astype(bf16)
    taps = s.conv_weight[...].reshape(4, 512).astype(f32)
    taps = jnp.concatenate([taps, jnp.zeros((4, 512), f32)], axis=0).T
    for tap in range(4):
        s.taps[tap] = jnp.broadcast_to(taps[:, tap:tap + 1], (512, T))
    block = iota((32, T), 0)
    start = jnp.int32(0)
    hit = jnp.zeros((32, T), f32)
    for q in range(8):
        hit = jnp.where(block == start, 1.0, hit)
        start = start + s.req_blocks[0, q]
    s.stay[...] = 1.0 - hit

def setup_gates(s):
    lane = iota((NC, T), 1)
    for r in range(2):
        x = s.aux[:, r, :] + s.dt_bias[r]
        rate = jnp.exp(jnp.full((NC, T), s.a_log[r], f32))
        decay = -rate * (jnp.maximum(x, 0.0) + jnp.log1p(jnp.exp(-jnp.abs(x))))
        c = decay
        for sh in (1, 2, 4, 8, 16, 32):
            c = c + jnp.where(lane % SPAN >= sh, pltpu.roll(c, sh, 1), 0.0)
        end0 = jnp.broadcast_to(c[:, SPAN - 1:SPAN], (NC, T))
        end1 = jnp.broadcast_to(c[:, T - 1:T], (NC, T))
        s.cum[r] = c
        s.fade[r] = jnp.exp(jnp.where(lane < SPAN, end0, end1) - c)
        s.lift[r] = jnp.exp(c)
        s.beta[r] = 1.0 / (1.0 + jnp.exp(-s.aux[:, 2 + r, :]))
        s.keep[r, 0] = jnp.exp(end0)
        s.keep[r, 1] = jnp.exp(end1)

def row(ref, c):
    return ref[pl.ds(c, 1), :]

def read_chunk(s, c):
    before = lax.rem(c + NC - 1, NC)
    lane = iota((1, T), 1)
    token = lane + c * T
    start = jnp.int32(0)
    since = token
    for q in range(7):
        start = start + s.req_blocks[0, q] * SPAN
        since = jnp.where(token >= start, token - start, since)
    now = s.x[c]
    old = s.x[before]
    parts = []
    for g in range(4):
        rows = slice(g * T, (g + 1) * T)
        cur = now[rows].astype(f32)
        prev = old[rows].astype(f32)
        total = s.taps[3, rows, :] * cur
        for back in (1, 2, 3):
            moved = pltpu.roll(jnp.where(lane >= T - back, prev, cur), back, 1)
            total = total + s.taps[3 - back, rows, :] * jnp.where(since >= back, moved, 0.0)
        parts.append((total / (1.0 + jnp.exp(-total))).astype(bf16))
    qT = parts[0]
    kw = parts[1].astype(f32)
    kT = (kw * lax.rsqrt(jnp.sum(kw * kw, axis=0, keepdims=True) + 1e-6)).astype(bf16)
    k = kT.astype(f32).T.astype(bf16)
    both = dot(k, jnp.concatenate([kT, qT], axis=1))
    gram, raw = both[:, :T], both[:, T:]
    minus = []
    for r in range(2):
        cum = row(s.cum.at[r], c)
        col = jnp.broadcast_to(cum, (T, T)).T
        e = jnp.exp((cum - col) * s.seen[...]) * s.seen[...]
        s.score[c, r] = (raw * e).astype(bf16)
        minus.append(gram * e * (s.later[...] * row(s.beta.at[r], c)))
    j, i = iota((16, T), 0), iota((16, T), 1)
    pick = jnp.where((j % 8 < 3) & (i == (j // 8) * SPAN + SPAN - 3 + j % 8), 1.0, 0.0).astype(bf16)
    tails = dot_nt(pick, now)
    s.tails[2 * c] = tails[:8]
    s.tails[2 * c + 1] = tails[8:]
    return qT, kT, k, parts[2:], minus


def solve(s, minus):
    low = [n.astype(bf16) for n in minus]
    count = range(len(minus))
    u = [(s.eye[...] - n * s.level[0].astype(f32)).astype(bf16) for n in minus]
    for level in range(1, 6):
        p = [dot(u[m], low[m] * s.level[level]).astype(bf16) for m in count]
        u = [u[m] - dot(p[m], u[m]).astype(bf16) for m in count]
    rest = [(minus[m] - low[m].astype(f32)).astype(bf16) for m in count]
    nx = [dot(jnp.concatenate([low[m], rest[m]], axis=0), u[m]) for m in count]
    res = [(s.eye[...] - u[m].astype(f32) - (nx[m][:T] + nx[m][T:])).astype(bf16) for m in count]
    return [(u[m].astype(f32) + dot(u[m], res[m])).astype(bf16) for m in count]


def weigh(s, chunks, data, u):
    zero = jnp.zeros((SPAN, T), bf16)
    pairs = [(m, r) for m in range(len(chunks)) for r in range(2)]
    kk, left, fade, stay, keep0, keep1 = [], [], [], [], [], []
    for m, c in enumerate(chunks):
        qT, kT, k, values, _ = data[m]
        kk.append(jnp.concatenate([
            jnp.concatenate([k[:SPAN], zero], axis=0),
            jnp.concatenate([zero, k[SPAN:]], axis=0)], axis=1))
        for r in range(2):
            beta = row(s.beta.at[r], c)
            sk = (kT.astype(f32) * (beta * row(s.lift.at[r], c))).astype(bf16)
            sv = (values[r].astype(f32) * beta).astype(bf16)
            left.append(jnp.concatenate([sv, sk], axis=0))
            fade.append(row(s.fade.at[r], c))
            stay.append(row(s.stay, 2 * c + 1))
            keep0.append(row(s.keep.at[r, 0], c))
            keep1.append(row(s.keep.at[r, 1], c))
    w = [dot(left[n], u[n]) for n in range(len(pairs))]
    gw = [dot((w[n] * fade[n]).astype(bf16), kk[m]) for n, (m, r) in enumerate(pairs)]
    joined = [g[:, :T].astype(bf16) for g in gw]
    both = [dot(joined[n], gw[n][T:, T:].astype(bf16)) for n in range(len(pairs))]
    for n, (m, r) in enumerate(pairs):
        c, g = chunks[m], gw[n]
        wb = w[n].astype(bf16)
        s.wv[c, r] = wb[:T]
        s.wq[c, r, :, :T] = wb[T:]
        s.wq[c, r, :, T:] = data[m][0]
        s.add[c, r, 0] = g[:T, :T]
        s.add[c, r, 1] = g[:T, T:] + stay[n] * (keep1[n] * g[:T, :T] - both[n][:T])
        s.turn[c, r, :, :T] = joined[n][T:]
        s.turn[c, r, :, T:] = (stay[n] * (keep1[n] * g[T:, :T] + keep0[n] * g[T:, T:] - both[n][T:])).astype(bf16)


def prep_chunks(s, chunks):
    data = [read_chunk(s, c) for c in chunks]
    minus = [n for d in data for n in d[4]]
    u = solve(s, minus)
    weigh(s, chunks, data, u)

def scan_blocks(s):
    def step(c, carry):
        state = list(carry)
        stay0, stay1 = row(s.stay, 2 * c), row(s.stay, 2 * c + 1)
        for r in range(2):
            keep0, keep1 = row(s.keep.at[r, 0], c), row(s.keep.at[r, 1], c)
            inside = state[r] * stay0
            low = inside.astype(bf16)
            moved = dot(low, s.turn[c, r])
            state[r] = (stay1 * keep0 * keep1 * inside + s.add[c, r, 1]) - moved[:, T:]
            middle = (keep0 * inside + s.add[c, r, 0]) - moved[:, :T]
            s.enter[c, r, :T, :] = low
            s.enter[c, r, T:, :] = (middle * stay1).astype(bf16)
            s.leave[2 * c, r] = middle.astype(bf16)
            s.leave[2 * c + 1, r] = state[r].astype(bf16)
        return tuple(state)

    zero = jnp.zeros((T, T), f32)
    lax.fori_loop(0, NC, step, (zero, zero))


def post_chunks(s, chunks):
    first = iota((1, T), 1) < SPAN
    pairs = [(c, r) for c in chunks for r in range(2)]
    both = [dot(s.enter[c, r], s.wq[c, r]) for c, r in pairs]
    new = [(s.wv[c, r].astype(f32) - jnp.where(first, x[:T, :T], x[T:, :T])).astype(bf16)
           for (c, r), x in zip(pairs, both)]
    old = [row(s.lift.at[r], c) * jnp.where(first, x[:T, T:], x[T:, T:]) for (c, r), x in zip(pairs, both)]
    out = [(old[n] + dot(new[n], s.score[c, r])).astype(bf16) for n, (c, r) in enumerate(pairs)]
    for n, (c, r) in enumerate(pairs):
        s.core[c, r * T:(r + 1) * T, :] = out[n]


SCRATCH = dict(
    x=((NC, 512, T), bf16), aux=((NC, 8, T), f32),
    cum=((2, NC, T), f32), fade=((2, NC, T), f32), lift=((2, NC, T), f32), beta=((2, NC, T), f32),
    keep=((2, 2, NC, T), f32), stay=((32, T), f32),
    seen=((T, T), f32), later=((T, T), f32), eye=((T, T), f32), level=((6, T, T), bf16),
    taps=((4, 512, T), f32),
    wv=((NC, 2, T, T), bf16), wq=((NC, 2, T, 2 * T), bf16), score=((NC, 2, T, T), bf16),
    add=((NC, 2, 2, T, T), f32), turn=((NC, 2, T, 2 * T), bf16),
    enter=((NC, 2, 2 * T, T), bf16), leave=((32, 2, T, T), bf16),
    core=((NC, 256, T), bf16), tails=((32, 8, 512), f32),
)

class Refs:
    pass


N_SEQ, N_REP, REQS, CAP = 16, 8, 8, 2
AHEAD = 11
BEFORE = 4
FIRST = False
VMEM_GRANT = 63 << 20
MESH = pl.DeviceIdType.MESH
VMEM = pl.BlockSpec(memory_space=pltpu.VMEM)
SMEM = pl.BlockSpec(memory_space=pltpu.SMEM)
HBM = pl.BlockSpec(memory_space=pltpu.MemorySpace.HBM)
SCRATCH_NAMES = list(SCRATCH)


def fill_slots(s):
    keys, lasts = [], []
    last = jnp.int32(-1)
    for q in range(REQS):
        last = last + s.req_blocks[0, q]
        rank = jnp.int32(0)
        for p in range(q):
            hit = (s.replica_of[0, p] == s.replica_of[0, q]) & (s.finished[0, p] > 0)
            rank = rank + jnp.where(hit, 1, 0)
        keys.append(jnp.where(s.finished[0, q] > 0, s.replica_of[0, q] * CAP + rank, -1))
        lasts.append(last)
    for m in range(N_REP * CAP):
        where, used = jnp.int32(0), jnp.int32(0)
        for q in range(REQS):
            where = where + jnp.where(keys[q] == m, lasts[q], 0)
            used = used + jnp.where(keys[q] == m, 1, 0)
        s.slot_block[m] = where
        s.slot_used[m] = used


def build_slot(s, d, k):
    m = d * CAP + k
    block, used = s.slot_block[m], s.slot_used[m].astype(f32)
    for r in range(2):
        flipped = dot_nt(s.eye[...].astype(bf16), s.leave[block, r])
        s.out_states[d, k, r] = (flipped * used).astype(bf16)
    count = (s.slot_used[d * CAP] + s.slot_used[d * CAP + 1]).astype(f32)
    rows = s.tails[block] * used
    return jnp.where(iota((8, 512), 0) == 3, count, rows)


ORDER = (1, 15, 4, 12, 5, 11, 3, 13, 2, 14, 6, 10, 8, 7, 9)
GROUPS = ((1, 0, 5, 12), (4, 13, 2, 15), (3, 14, 6, 11), (7, 10, 8, 9))
READY = (0, 6, 10, 12, 15)
REP_ORDER = (2, 6, 1, 7, 3, 5, 4, 0)


def entry(table, i):
    out = jnp.int32(table[0])
    for t in range(1, len(table)):
        out = jnp.where(i == t, table[t], out)
    return out


def main_kernel(mixed, decay_in, beta_in, conv_weight, a_log, dt_bias, req_blocks, replica_of, finished,
                back, got_states, got_tails, *scratch):
    s = Refs()
    names = SCRATCH_NAMES + [
        "aux_out", "out_states", "out_tails", "slot_block", "slot_used",
        "x_send", "x_recv", "aux_send", "aux_recv", "core_send", "core_recv",
        "st_send", "st_recv", "tl_send", "tl_recv", "own",
        "decay_in", "beta_in", "conv_weight", "a_log", "dt_bias", "req_blocks", "replica_of", "finished", "small"]
    for name, ref in zip(names, scratch):
        setattr(s, name, ref)
    me, rep = lax.axis_index("seq"), lax.axis_index("rep")

    barrier = pltpu.get_barrier_semaphore()
    for k in range(1, N_SEQ):
        pl.semaphore_signal(barrier, inc=1, device_id={"seq": lax.rem(me + k, N_SEQ)}, device_id_type=MESH)
    for k in range(1, N_REP):
        pl.semaphore_signal(barrier, inc=1, device_id={"rep": lax.rem(rep + k, N_REP)}, device_id_type=MESH)
    small = [
        pltpu.make_async_copy(source, target, s.small.at[n]) for n, (source, target) in enumerate((
            (decay_in, s.decay_in), (beta_in, s.beta_in), (conv_weight, s.conv_weight), (a_log, s.a_log),
            (dt_bias, s.dt_bias), (req_blocks, s.req_blocks), (replica_of, s.replica_of), (finished, s.finished)))]
    for copy in small:
        copy.start()
    own_x = pltpu.make_async_copy(mixed.at[0, me], s.x.at[me], s.own.at[0])
    own_x.start()

    def aux_copy(k):
        to = lax.rem(me + N_SEQ - k, N_SEQ)
        return pltpu.make_async_remote_copy(
            src_ref=s.aux_out.at[to], dst_ref=s.aux.at[me], send_sem=s.aux_send.at[k], recv_sem=s.aux_recv.at[k],
            device_id={"seq": to}, device_id_type=MESH)

    def x_copy(k):
        to = lax.rem(me + N_SEQ - k, N_SEQ)
        return pltpu.make_async_remote_copy(
            src_ref=mixed.at[0, to], dst_ref=s.x.at[me], send_sem=s.x_send.at[k], recv_sem=s.x_recv.at[k],
            device_id={"seq": to}, device_id_type=MESH)

    def start_aux(k, carry):
        aux_copy(k).start()
        return carry

    pl.semaphore_wait(barrier, N_SEQ + N_REP - 2)
    for n in range(BEFORE):
        x_copy(ORDER[n]).start()
    for copy in small:
        copy.wait()
    for h in range(N_SEQ):
        s.aux_out[h, 0:2, :] = s.decay_in[0, h].astype(f32)
        s.aux_out[h, 2:4, :] = s.beta_in[0, h].astype(f32)
        s.aux_out[h, 4:8, :] = jnp.zeros((4, T), f32)

    own_aux = pltpu.make_async_copy(s.aux_out.at[me], s.aux.at[me], s.own.at[1])
    own_aux.start()
    lax.fori_loop(1, N_SEQ, start_aux, 0)
    for n in range(BEFORE, AHEAD):
        x_copy(ORDER[n]).start()
    setup_tables(s)
    fill_slots(s)
    own_x.wait()
    own_aux.wait()

    def wait_aux(k, carry):
        aux_copy(k).wait_recv()
        return carry

    lax.fori_loop(1, N_SEQ, wait_aux, 0)
    setup_gates(s)

    def prep(g, carry):
        for n in range(4):
            @pl.when(g == n)
            def _(n=n):
                for m in range(READY[n], READY[n + 1]):
                    x_copy(ORDER[m]).wait_recv()
                    if m + AHEAD < N_SEQ - 1:
                        x_copy(ORDER[m + AHEAD]).start()

        prep_chunks(s, [lax.rem(me + entry([group[t] for group in GROUPS], g), N_SEQ) for t in range(4)])
        return carry

    lax.fori_loop(0, 4, prep, 0)
    scan_blocks(s)

    def core_copy(k):
        to = lax.rem(me + k, N_SEQ)
        return pltpu.make_async_remote_copy(
            src_ref=s.core.at[to], dst_ref=back.at[me], send_sem=s.core_send.at[k], recv_sem=s.core_recv.at[k],
            device_id={"seq": to}, device_id_type=MESH)

    def state_copies(k):
        to = lax.rem(rep + k, N_REP)
        return [
            pltpu.make_async_remote_copy(
                src_ref=s.out_states.at[to], dst_ref=got_states.at[rep], send_sem=s.st_send.at[k],
                recv_sem=s.st_recv.at[k], device_id={"rep": to}, device_id_type=MESH),
            pltpu.make_async_remote_copy(
                src_ref=s.out_tails.at[to], dst_ref=got_tails.at[rep], send_sem=s.tl_send.at[k],
                recv_sem=s.tl_recv.at[k], device_id={"rep": to}, device_id_type=MESH)]

    def hand_off(g):
        for t in range(2):
            k = entry([REP_ORDER[2 * n + t] for n in range(4)], g)
            d = lax.rem(rep + k, N_REP)
            tails = [build_slot(s, d, slot) for slot in range(CAP)]
            s.out_tails[d] = jnp.concatenate(tails, axis=0).astype(bf16)

            @pl.when(k > 0)
            def _(k=k):
                for copy in state_copies(k):
                    copy.start()

    def post(g, carry):
        steps = [entry([(ORDER + (0,))[4 * n + t] for n in range(4)], g) for t in range(4)]
        post_chunks(s, [lax.rem(me + k, N_SEQ) for k in steps])
        for t in range(4):
            @pl.when(steps[t] > 0)
            def _(t=t):
                core_copy(steps[t]).start()

        if not FIRST:
            hand_off(g)
        return carry

    def hand_off_first(g, carry):
        hand_off(g)
        return carry

    if FIRST:
        lax.fori_loop(0, 4, hand_off_first, 0)
    lax.fori_loop(0, 4, post, 0)
    own = [
        pltpu.make_async_copy(s.core.at[me], back.at[me], s.own.at[2]),
        pltpu.make_async_copy(s.out_states.at[rep], got_states.at[rep], s.own.at[3]),
        pltpu.make_async_copy(s.out_tails.at[rep], got_tails.at[rep], s.own.at[4])]
    for copy in own:
        copy.start()

    def finish_seq(k, carry):
        aux_copy(k).wait_send()
        x_copy(k).wait_send()
        core_copy(k).wait()
        return carry

    def finish_rep(k, carry):
        for copy in state_copies(k):
            copy.wait()
        return carry

    lax.fori_loop(1, N_SEQ, finish_seq, 0)
    lax.fori_loop(1, N_REP, finish_rep, 0)
    for copy in own:
        copy.wait()


def finish_kernel(back_hbm, gate, gain_hbm, got_states_hbm, got_tails_hbm, mixer, states, tails_out,
                  z_in, mixed_out, states_out, back, gain, got_states, got_tails, tails,
                  gate_sem, back_sem, mixer_sem, states_sem, load_sem):
    first = [
        pltpu.make_async_copy(got_tails_hbm, got_tails, load_sem.at[0]),
        pltpu.make_async_copy(got_states_hbm, got_states, load_sem.at[1]),
        pltpu.make_async_copy(gain_hbm, gain, load_sem.at[2])]

    def load(h):
        return [
            pltpu.make_async_copy(gate.at[0, h], z_in.at[h], gate_sem.at[h]),
            pltpu.make_async_copy(back_hbm.at[h], back.at[h], back_sem.at[h])]

    for copy in first:
        copy.start()
    for h in range(N_SEQ):
        for copy in load(h):
            copy.start()
    for copy in first:
        copy.wait()
    counts = [jnp.max(got_tails[q, 0:8, 0:T].astype(f32)[3:4]).astype(jnp.int32) for q in range(N_REP)]
    bases, base = [], jnp.int32(0)
    for q in range(N_REP):
        bases.append(base)
        base = base + counts[q]

    def store_states(slot):
        return pltpu.make_async_copy(states_out.at[slot], states.at[0, slot], states_sem.at[slot])

    def store_mixer(h):
        return pltpu.make_async_copy(mixed_out.at[h], mixer.at[0, h], mixer_sem.at[h])

    def land(slot):
        pick, used = jnp.int32(0), jnp.int32(0)
        for q in range(N_REP):
            rank = slot - bases[q]
            hit = (rank >= 0) & (rank < counts[q])
            pick = jnp.where(hit, q * CAP + rank, pick)
            used = jnp.where(hit, 1, used)
        scale = used.astype(f32)
        source, rank = pick // CAP, pick % CAP
        for r in range(2):
            states_out[slot, r] = got_states[source, rank, r].astype(f32) * scale
        store_states(slot).start()
        both = got_tails[source].astype(f32)
        rows = jnp.where(rank == 0, both[0:8], both[8:16]) * scale
        for p in range(3):
            tails[p, pl.ds(slot, 1), :] = rows[p:p + 1]

    def land_some(g, carry):
        for t in range(4):
            land(g * 4 + t)
        return carry

    lax.fori_loop(0, N_REP * CAP // 4, land_some, 0)
    tails_out[...] = tails[...].astype(bf16)
    column = jnp.broadcast_to(gain[...], (T, T)).T

    def norm(g, carry):
        for t in range(4):
            for copy in load(g * 4 + t):
                copy.wait()
        for t in range(4):
            h = g * 4 + t
            for r in range(2):
                rows = slice(r * T, (r + 1) * T)
                value = back[h, rows, :].astype(f32)
                inverse = lax.rsqrt(jnp.mean(value * value, axis=0, keepdims=True) + 1e-6)
                z = z_in[h, rows, :].astype(f32)
                mixed_out[h, rows, :] = (value * inverse * column * (z / (1.0 + jnp.exp(-z)))).astype(bf16)
        for t in range(4):
            store_mixer(g * 4 + t).start()
        return carry

    lax.fori_loop(0, N_SEQ // 4, norm, 0)

    def drain(h, carry):
        store_states(h).wait()
        store_mixer(h).wait()
        return carry

    lax.fori_loop(0, N_SEQ, drain, 0)


def finish_call(*operands):
    dma = pltpu.SemaphoreType.DMA
    return pl.pallas_call(
        finish_kernel,
        name="finish",
        out_shape=[
            jax.ShapeDtypeStruct((1, N_SEQ, 2 * T, T), bf16),
            jax.ShapeDtypeStruct((1, N_REP * CAP, 2, T, T), f32),
            jax.ShapeDtypeStruct((3, N_REP * CAP, 512), bf16)],
        in_specs=[HBM] * 5,
        out_specs=[HBM, HBM, VMEM],
        scratch_shapes=[
            pltpu.VMEM((N_SEQ, 2 * T, T), bf16),
            pltpu.VMEM((N_SEQ, 2 * T, T), bf16),
            pltpu.VMEM((N_REP * CAP, 2, T, T), f32),
            pltpu.VMEM((N_SEQ, 2 * T, T), bf16),
            pltpu.VMEM((1, T), f32),
            pltpu.VMEM((N_REP, CAP, 2, T, T), bf16),
            pltpu.VMEM((N_REP, 16, 512), bf16),
            pltpu.VMEM((3, N_REP * CAP, 512), f32),
            dma((N_SEQ,)), dma((N_SEQ,)), dma((N_SEQ,)), dma((N_REP * CAP,)), dma((3,))],
        compiler_params=pltpu.CompilerParams(vmem_limit_bytes=VMEM_GRANT),
    )(*operands)


def body(mixed, decay_in, beta_in, gate_z, conv_weight, a_log, dt_bias, norm_gain, req_blocks, replica_of, finished):
    dma = pltpu.SemaphoreType.DMA
    back, got_states, got_tails = pl.pallas_call(
        main_kernel,
        name="main",
        out_shape=[
            jax.ShapeDtypeStruct((N_SEQ, 2 * T, T), bf16),
            jax.ShapeDtypeStruct((N_REP, CAP, 2, T, T), bf16),
            jax.ShapeDtypeStruct((N_REP, 16, 512), bf16)],
        in_specs=[HBM] * 9,
        out_specs=[HBM] * 3,
        scratch_shapes=[pltpu.VMEM(*SCRATCH[name]) for name in SCRATCH_NAMES] + [
            pltpu.VMEM((N_SEQ, 8, T), f32),
            pltpu.VMEM((N_REP, CAP, 2, T, T), bf16),
            pltpu.VMEM((N_REP, 16, 512), bf16),
            pltpu.SMEM((N_REP * CAP,), jnp.int32),
            pltpu.SMEM((N_REP * CAP,), jnp.int32)] + [dma((N_SEQ,))] * 6 + [dma((N_REP,))] * 4 + [
                dma((5,)),
                pltpu.VMEM(decay_in.shape, bf16), pltpu.VMEM(beta_in.shape, bf16), pltpu.VMEM((1, 4, 512), bf16),
                pltpu.SMEM(a_log.shape, f32), pltpu.SMEM(dt_bias.shape, f32), pltpu.SMEM(req_blocks.shape, jnp.int32),
                pltpu.SMEM(replica_of.shape, jnp.int32), pltpu.SMEM(finished.shape, jnp.int32), dma((8,))],
        compiler_params=pltpu.CompilerParams(
            collective_id=0, has_side_effects=True, vmem_limit_bytes=VMEM_GRANT),
    )(mixed, decay_in, beta_in, jnp.transpose(conv_weight, (1, 0, 2)), a_log, dt_bias, req_blocks, replica_of, finished)
    mixer, states, tails = finish_call(back, gate_z, norm_gain.reshape(1, T), got_states, got_tails)
    tails = jnp.transpose(tails, (1, 0, 2))[None, :, :, None, :]
    return mixer, states, tails


def solution(mesh):
    placed = P("rep", None, None, "seq")
    return jax.shard_map(
        body,
        mesh=mesh,
        in_specs=(placed, placed, placed, placed, P(None, "seq", None), P("seq"), P("seq"), P(),
                  P("rep", None), P("rep", None), P("rep", None)),
        out_specs=(placed, P("rep", None, "seq", None, None), P("rep", None, None, "seq", None)),
        check_vma=False,
    )
```

```python
import jax
import jax.numpy as jnp
from jax import lax
from jax.experimental import pallas as pl
from jax.experimental.pallas import tpu as pltpu
from jax.sharding import PartitionSpec as P

f32, bf16 = jnp.float32, jnp.bfloat16
NC, T, SPAN = 16, 128, 64

def dot(a, b):
    return jnp.dot(a, b, preferred_element_type=f32)

def dot_nt(a, b):
    return lax.dot_general(a, b, (((1,), (1,)), ((), ())), preferred_element_type=f32)

def iota(shape, d):
    return lax.broadcasted_iota(jnp.int32, shape, d)

def setup_tables(s):
    j, i = iota((T, T), 0), iota((T, T), 1)
    same = (j // SPAN) == (i // SPAN)
    s.seen[...] = jnp.where(same & (j <= i), 1.0, 0.0)
    s.later[...] = jnp.where(same & (j < i), 1.0, 0.0)
    s.eye[...] = jnp.where(j == i, 1.0, 0.0)
    for level in range(6):
        s.level[level] = jnp.where(((j ^ i) >> level) == 1, 1.0, 0.0).astype(bf16)
    taps = s.conv_weight[...].reshape(4, 512).astype(f32)
    taps = jnp.concatenate([taps, jnp.zeros((4, 512), f32)], axis=0).T
    for tap in range(4):
        s.taps[tap] = jnp.broadcast_to(taps[:, tap:tap + 1], (512, T))
    block = iota((32, T), 0)
    start = jnp.int32(0)
    hit = jnp.zeros((32, T), f32)
    for q in range(8):
        hit = jnp.where(block == start, 1.0, hit)
        start = start + s.req_blocks[0, q]
    s.stay[...] = 1.0 - hit

def setup_gates(s):
    lane = iota((NC, T), 1)
    for r in range(2):
        x = s.aux[:, r, :] + s.dt_bias[r]
        rate = jnp.exp(jnp.full((NC, T), s.a_log[r], f32))
        decay = -rate * (jnp.maximum(x, 0.0) + jnp.log1p(jnp.exp(-jnp.abs(x))))
        c = decay
        for sh in (1, 2, 4, 8, 16, 32):
            c = c + jnp.where(lane % SPAN >= sh, pltpu.roll(c, sh, 1), 0.0)
        end0 = jnp.broadcast_to(c[:, SPAN - 1:SPAN], (NC, T))
        end1 = jnp.broadcast_to(c[:, T - 1:T], (NC, T))
        s.cum[r] = c
        s.fade[r] = jnp.exp(jnp.where(lane < SPAN, end0, end1) - c)
        s.lift[r] = jnp.exp(c)
        s.beta[r] = 1.0 / (1.0 + jnp.exp(-s.aux[:, 2 + r, :]))
        s.keep[r, 0] = jnp.exp(end0)
        s.keep[r, 1] = jnp.exp(end1)

def row(ref, c):
    return ref[pl.ds(c, 1), :]

def read_chunk(s, c):
    before = lax.rem(c + NC - 1, NC)
    lane = iota((1, T), 1)
    token = lane + c * T
    start = jnp.int32(0)
    since = token
    for q in range(7):
        start = start + s.req_blocks[0, q] * SPAN
        since = jnp.where(token >= start, token - start, since)
    now = s.x[c]
    old = s.x[before]
    parts = []
    for g in range(4):
        rows = slice(g * T, (g + 1) * T)
        cur = now[rows].astype(f32)
        prev = old[rows].astype(f32)
        total = s.taps[3, rows, :] * cur
        for back in (1, 2, 3):
            moved = pltpu.roll(jnp.where(lane >= T - back, prev, cur), back, 1)
            total = total + s.taps[3 - back, rows, :] * jnp.where(since >= back, moved, 0.0)
        parts.append((total / (1.0 + jnp.exp(-total))).astype(bf16))
    qT = parts[0]
    kw = parts[1].astype(f32)
    kT = (kw * lax.rsqrt(jnp.sum(kw * kw, axis=0, keepdims=True) + 1e-6)).astype(bf16)
    k = kT.astype(f32).T.astype(bf16)
    both = dot(k, jnp.concatenate([kT, qT], axis=1))
    gram, raw = both[:, :T], both[:, T:]
    minus = []
    for r in range(2):
        cum = row(s.cum.at[r], c)
        col = jnp.broadcast_to(cum, (T, T)).T
        e = jnp.exp((cum - col) * s.seen[...]) * s.seen[...]
        s.score[c, r] = (raw * e).astype(bf16)
        minus.append(gram * e * (s.later[...] * row(s.beta.at[r], c)))
    j, i = iota((16, T), 0), iota((16, T), 1)
    pick = jnp.where((j % 8 < 3) & (i == (j // 8) * SPAN + SPAN - 3 + j % 8), 1.0, 0.0).astype(bf16)
    tails = dot_nt(pick, now)
    s.tails[2 * c] = tails[:8]
    s.tails[2 * c + 1] = tails[8:]
    return qT, kT, k, parts[2:], minus


def solve(s, minus):
    low = [n.astype(bf16) for n in minus]
    count = range(len(minus))
    u = [(s.eye[...] - n * s.level[0].astype(f32)).astype(bf16) for n in minus]
    for level in range(1, 6):
        p = [dot(u[m], low[m] * s.level[level]).astype(bf16) for m in count]
        u = [u[m] - dot(p[m], u[m]).astype(bf16) for m in count]
    rest = [(minus[m] - low[m].astype(f32)).astype(bf16) for m in count]
    nx = [dot(jnp.concatenate([low[m], rest[m]], axis=0), u[m]) for m in count]
    res = [(s.eye[...] - u[m].astype(f32) - (nx[m][:T] + nx[m][T:])).astype(bf16) for m in count]
    return [(u[m].astype(f32) + dot(u[m], res[m])).astype(bf16) for m in count]


def weigh(s, chunks, data, u):
    zero = jnp.zeros((SPAN, T), bf16)
    pairs = [(m, r) for m in range(len(chunks)) for r in range(2)]
    kk, left, fade, stay, keep0, keep1 = [], [], [], [], [], []
    for m, c in enumerate(chunks):
        qT, kT, k, values, _ = data[m]
        kk.append(jnp.concatenate([
            jnp.concatenate([k[:SPAN], zero], axis=0),
            jnp.concatenate([zero, k[SPAN:]], axis=0)], axis=1))
        for r in range(2):
            beta = row(s.beta.at[r], c)
            sk = (kT.astype(f32) * (beta * row(s.lift.at[r], c))).astype(bf16)
            sv = (values[r].astype(f32) * beta).astype(bf16)
            left.append(jnp.concatenate([sv, sk], axis=0))
            fade.append(row(s.fade.at[r], c))
            stay.append(row(s.stay, 2 * c + 1))
            keep0.append(row(s.keep.at[r, 0], c))
            keep1.append(row(s.keep.at[r, 1], c))
    w = [dot(left[n], u[n]) for n in range(len(pairs))]
    gw = [dot((w[n] * fade[n]).astype(bf16), kk[m]) for n, (m, r) in enumerate(pairs)]
    joined = [g[:, :T].astype(bf16) for g in gw]
    both = [dot(joined[n], gw[n][T:, T:].astype(bf16)) for n in range(len(pairs))]
    for n, (m, r) in enumerate(pairs):
        c, g = chunks[m], gw[n]
        wb = w[n].astype(bf16)
        s.wv[c, r] = wb[:T]
        s.wq[c, r, :, :T] = wb[T:]
        s.wq[c, r, :, T:] = data[m][0]
        s.add[c, r, 0] = g[:T, :T]
        s.add[c, r, 1] = g[:T, T:] + stay[n] * (keep1[n] * g[:T, :T] - both[n][:T])
        s.turn[c, r, :, :T] = joined[n][T:]
        s.turn[c, r, :, T:] = (stay[n] * (keep1[n] * g[T:, :T] + keep0[n] * g[T:, T:] - both[n][T:])).astype(bf16)


def prep_chunks(s, chunks):
    data = [read_chunk(s, c) for c in chunks]
    minus = [n for d in data for n in d[4]]
    u = solve(s, minus)
    weigh(s, chunks, data, u)

def scan_blocks(s):
    def step(c, carry):
        state = list(carry)
        stay0, stay1 = row(s.stay, 2 * c), row(s.stay, 2 * c + 1)
        for r in range(2):
            keep0, keep1 = row(s.keep.at[r, 0], c), row(s.keep.at[r, 1], c)
            inside = state[r] * stay0
            low = inside.astype(bf16)
            moved = dot(low, s.turn[c, r])
            state[r] = (stay1 * keep0 * keep1 * inside + s.add[c, r, 1]) - moved[:, T:]
            middle = (keep0 * inside + s.add[c, r, 0]) - moved[:, :T]
            s.enter[c, r, :T, :] = low
            s.enter[c, r, T:, :] = (middle * stay1).astype(bf16)
            s.leave[2 * c, r] = middle.astype(bf16)
            s.leave[2 * c + 1, r] = state[r].astype(bf16)
        return tuple(state)

    zero = jnp.zeros((T, T), f32)
    lax.fori_loop(0, NC, step, (zero, zero))


def post_chunks(s, chunks):
    first = iota((1, T), 1) < SPAN
    pairs = [(c, r) for c in chunks for r in range(2)]
    both = [dot(s.enter[c, r], s.wq[c, r]) for c, r in pairs]
    new = [(s.wv[c, r].astype(f32) - jnp.where(first, x[:T, :T], x[T:, :T])).astype(bf16)
           for (c, r), x in zip(pairs, both)]
    old = [row(s.lift.at[r], c) * jnp.where(first, x[:T, T:], x[T:, T:]) for (c, r), x in zip(pairs, both)]
    out = [(old[n] + dot(new[n], s.score[c, r])).astype(bf16) for n, (c, r) in enumerate(pairs)]
    for n, (c, r) in enumerate(pairs):
        s.core[c, r * T:(r + 1) * T, :] = out[n]


SCRATCH = dict(
    x=((NC, 512, T), bf16), aux=((NC, 8, T), f32),
    cum=((2, NC, T), f32), fade=((2, NC, T), f32), lift=((2, NC, T), f32), beta=((2, NC, T), f32),
    keep=((2, 2, NC, T), f32), stay=((32, T), f32),
    seen=((T, T), f32), later=((T, T), f32), eye=((T, T), f32), level=((6, T, T), bf16),
    taps=((4, 512, T), f32),
    wv=((NC, 2, T, T), bf16), wq=((NC, 2, T, 2 * T), bf16), score=((NC, 2, T, T), bf16),
    add=((NC, 2, 2, T, T), f32), turn=((NC, 2, T, 2 * T), bf16),
    enter=((NC, 2, 2 * T, T), bf16), leave=((32, 2, T, T), bf16),
    core=((NC, 256, T), bf16), tails=((32, 8, 512), f32),
)

class Refs:
    pass


N_SEQ, N_REP, REQS, CAP = 16, 8, 8, 2
AHEAD = 11
BEFORE = 4
FIRST = False
VMEM_GRANT = 63 << 20
MESH = pl.DeviceIdType.MESH
VMEM = pl.BlockSpec(memory_space=pltpu.VMEM)
SMEM = pl.BlockSpec(memory_space=pltpu.SMEM)
HBM = pl.BlockSpec(memory_space=pltpu.MemorySpace.HBM)
SCRATCH_NAMES = list(SCRATCH)


def fill_slots(s):
    keys, lasts = [], []
    last = jnp.int32(-1)
    for q in range(REQS):
        last = last + s.req_blocks[0, q]
        rank = jnp.int32(0)
        for p in range(q):
            hit = (s.replica_of[0, p] == s.replica_of[0, q]) & (s.finished[0, p] > 0)
            rank = rank + jnp.where(hit, 1, 0)
        keys.append(jnp.where(s.finished[0, q] > 0, s.replica_of[0, q] * CAP + rank, -1))
        lasts.append(last)
    for m in range(N_REP * CAP):
        where, used = jnp.int32(0), jnp.int32(0)
        for q in range(REQS):
            where = where + jnp.where(keys[q] == m, lasts[q], 0)
            used = used + jnp.where(keys[q] == m, 1, 0)
        s.slot_block[m] = where
        s.slot_used[m] = used


def build_slot(s, d, k):
    m = d * CAP + k
    block, used = s.slot_block[m], s.slot_used[m].astype(f32)
    for r in range(2):
        flipped = dot_nt(s.eye[...].astype(bf16), s.leave[block, r])
        s.out_states[d, k, r] = (flipped * used).astype(bf16)
    count = (s.slot_used[d * CAP] + s.slot_used[d * CAP + 1]).astype(f32)
    rows = s.tails[block] * used
    return jnp.where(iota((8, 512), 0) == 3, count, rows)


ORDER = (1, 15, 4, 12, 5, 11, 3, 13, 2, 14, 8, 6, 10, 7, 9)
GROUPS = ((1, 0, 5, 12), (4, 13, 2, 15), (3, 14, 6, 11), (7, 10, 8, 9))
READY = (0, 6, 10, 13, 15)
REP_ORDER = (2, 6, 1, 7, 3, 5, 4, 0)


def entry(table, i):
    out = jnp.int32(table[0])
    for t in range(1, len(table)):
        out = jnp.where(i == t, table[t], out)
    return out


def main_kernel(mixed, decay_in, beta_in, conv_weight, a_log, dt_bias, req_blocks, replica_of, finished,
                back, got_states, got_tails, *scratch):
    s = Refs()
    names = SCRATCH_NAMES + [
        "aux_out", "out_states", "out_tails", "slot_block", "slot_used",
        "x_send", "x_recv", "aux_send", "aux_recv", "core_send", "core_recv",
        "st_send", "st_recv", "tl_send", "tl_recv", "own",
        "decay_in", "beta_in", "conv_weight", "a_log", "dt_bias", "req_blocks", "replica_of", "finished", "small"]
    for name, ref in zip(names, scratch):
        setattr(s, name, ref)
    me, rep = lax.axis_index("seq"), lax.axis_index("rep")

    barrier = pltpu.get_barrier_semaphore()
    for k in range(1, N_SEQ):
        pl.semaphore_signal(barrier, inc=1, device_id={"seq": lax.rem(me + k, N_SEQ)}, device_id_type=MESH)
    for k in range(1, N_REP):
        pl.semaphore_signal(barrier, inc=1, device_id={"rep": lax.rem(rep + k, N_REP)}, device_id_type=MESH)
    small = [
        pltpu.make_async_copy(source, target, s.small.at[n]) for n, (source, target) in enumerate((
            (decay_in, s.decay_in), (beta_in, s.beta_in), (conv_weight, s.conv_weight), (a_log, s.a_log),
            (dt_bias, s.dt_bias), (req_blocks, s.req_blocks), (replica_of, s.replica_of), (finished, s.finished)))]
    for copy in small:
        copy.start()
    own_x = pltpu.make_async_copy(mixed.at[0, me], s.x.at[me], s.own.at[0])
    own_x.start()

    def aux_copy(k):
        to = lax.rem(me + N_SEQ - k, N_SEQ)
        return pltpu.make_async_remote_copy(
            src_ref=s.aux_out.at[to], dst_ref=s.aux.at[me], send_sem=s.aux_send.at[k], recv_sem=s.aux_recv.at[k],
            device_id={"seq": to}, device_id_type=MESH)

    def x_copy(k):
        to = lax.rem(me + N_SEQ - k, N_SEQ)
        return pltpu.make_async_remote_copy(
            src_ref=mixed.at[0, to], dst_ref=s.x.at[me], send_sem=s.x_send.at[k], recv_sem=s.x_recv.at[k],
            device_id={"seq": to}, device_id_type=MESH)

    def start_aux(k, carry):
        aux_copy(k).start()
        return carry

    pl.semaphore_wait(barrier, N_SEQ + N_REP - 2)
    for n in range(BEFORE):
        x_copy(ORDER[n]).start()
    for copy in small:
        copy.wait()
    for h in range(N_SEQ):
        s.aux_out[h, 0:2, :] = s.decay_in[0, h].astype(f32)
        s.aux_out[h, 2:4, :] = s.beta_in[0, h].astype(f32)
        s.aux_out[h, 4:8, :] = jnp.zeros((4, T), f32)

    own_aux = pltpu.make_async_copy(s.aux_out.at[me], s.aux.at[me], s.own.at[1])
    own_aux.start()
    lax.fori_loop(1, N_SEQ, start_aux, 0)
    for n in range(BEFORE, AHEAD):
        x_copy(ORDER[n]).start()
    setup_tables(s)
    fill_slots(s)
    own_x.wait()
    own_aux.wait()

    def wait_aux(k, carry):
        aux_copy(k).wait_recv()
        return carry

    lax.fori_loop(1, N_SEQ, wait_aux, 0)
    setup_gates(s)

    def prep(g, carry):
        for n in range(4):
            @pl.when(g == n)
            def _(n=n):
                for m in range(READY[n], READY[n + 1]):
                    x_copy(ORDER[m]).wait_recv()
                    if m + AHEAD < N_SEQ - 1:
                        x_copy(ORDER[m + AHEAD]).start()

        prep_chunks(s, [lax.rem(me + entry([group[t] for group in GROUPS], g), N_SEQ) for t in range(4)])
        return carry

    lax.fori_loop(0, 4, prep, 0)
    scan_blocks(s)

    def core_copy(k):
        to = lax.rem(me + k, N_SEQ)
        return pltpu.make_async_remote_copy(
            src_ref=s.core.at[to], dst_ref=back.at[me], send_sem=s.core_send.at[k], recv_sem=s.core_recv.at[k],
            device_id={"seq": to}, device_id_type=MESH)

    def state_copies(k):
        to = lax.rem(rep + k, N_REP)
        return [
            pltpu.make_async_remote_copy(
                src_ref=s.out_states.at[to], dst_ref=got_states.at[rep], send_sem=s.st_send.at[k],
                recv_sem=s.st_recv.at[k], device_id={"rep": to}, device_id_type=MESH),
            pltpu.make_async_remote_copy(
                src_ref=s.out_tails.at[to], dst_ref=got_tails.at[rep], send_sem=s.tl_send.at[k],
                recv_sem=s.tl_recv.at[k], device_id={"rep": to}, device_id_type=MESH)]

    def hand_off(g):
        for t in range(2):
            k = entry([REP_ORDER[2 * n + t] for n in range(4)], g)
            d = lax.rem(rep + k, N_REP)
            tails = [build_slot(s, d, slot) for slot in range(CAP)]
            s.out_tails[d] = jnp.concatenate(tails, axis=0).astype(bf16)

            @pl.when(k > 0)
            def _(k=k):
                for copy in state_copies(k):
                    copy.start()

    def post(g, carry):
        steps = [entry([(ORDER + (0,))[4 * n + t] for n in range(4)], g) for t in range(4)]
        post_chunks(s, [lax.rem(me + k, N_SEQ) for k in steps])
        for t in range(4):
            @pl.when(steps[t] > 0)
            def _(t=t):
                core_copy(steps[t]).start()

        if not FIRST:
            hand_off(g)
        return carry

    def hand_off_first(g, carry):
        hand_off(g)
        return carry

    if FIRST:
        lax.fori_loop(0, 4, hand_off_first, 0)
    lax.fori_loop(0, 4, post, 0)
    own = [
        pltpu.make_async_copy(s.core.at[me], back.at[me], s.own.at[2]),
        pltpu.make_async_copy(s.out_states.at[rep], got_states.at[rep], s.own.at[3]),
        pltpu.make_async_copy(s.out_tails.at[rep], got_tails.at[rep], s.own.at[4])]
    for copy in own:
        copy.start()

    def finish_seq(k, carry):
        aux_copy(k).wait_send()
        x_copy(k).wait_send()
        core_copy(k).wait()
        return carry

    def finish_rep(k, carry):
        for copy in state_copies(k):
            copy.wait()
        return carry

    lax.fori_loop(1, N_SEQ, finish_seq, 0)
    lax.fori_loop(1, N_REP, finish_rep, 0)
    for copy in own:
        copy.wait()


def finish_kernel(back_hbm, gate, gain_hbm, got_states_hbm, got_tails_hbm, mixer, states, tails_out,
                  z_in, mixed_out, states_out, back, gain, got_states, got_tails, tails,
                  gate_sem, back_sem, mixer_sem, states_sem, load_sem):
    first = [
        pltpu.make_async_copy(got_tails_hbm, got_tails, load_sem.at[0]),
        pltpu.make_async_copy(got_states_hbm, got_states, load_sem.at[1]),
        pltpu.make_async_copy(gain_hbm, gain, load_sem.at[2])]

    def some(g):
        return pl.ds(4 * g, 4)

    def load(g):
        return [
            pltpu.make_async_copy(gate.at[0, some(g)], z_in.at[some(g)], gate_sem.at[g]),
            pltpu.make_async_copy(back_hbm.at[some(g)], back.at[some(g)], back_sem.at[g])]

    for copy in first:
        copy.start()
    for g in range(4):
        for copy in load(g):
            copy.start()
    for copy in first:
        copy.wait()
    counts = [jnp.max(got_tails[q, 0:8, 0:T].astype(f32)[3:4]).astype(jnp.int32) for q in range(N_REP)]
    bases, base = [], jnp.int32(0)
    for q in range(N_REP):
        bases.append(base)
        base = base + counts[q]

    def store_states(g):
        return pltpu.make_async_copy(states_out.at[some(g)], states.at[0, some(g)], states_sem.at[g])

    def store_mixer(g):
        return pltpu.make_async_copy(mixed_out.at[some(g)], mixer.at[0, some(g)], mixer_sem.at[g])

    def land(slot):
        pick, used = jnp.int32(0), jnp.int32(0)
        for q in range(N_REP):
            rank = slot - bases[q]
            hit = (rank >= 0) & (rank < counts[q])
            pick = jnp.where(hit, q * CAP + rank, pick)
            used = jnp.where(hit, 1, used)
        scale = used.astype(f32)
        source, rank = pick // CAP, pick % CAP
        for r in range(2):
            states_out[slot, r] = got_states[source, rank, r].astype(f32) * scale
        both = got_tails[source].astype(f32)
        rows = jnp.where(rank == 0, both[0:8], both[8:16]) * scale
        for p in range(3):
            tails[p, pl.ds(slot, 1), :] = rows[p:p + 1]

    def land_some(g, carry):
        for t in range(4):
            land(g * 4 + t)
        store_states(g).start()
        return carry

    lax.fori_loop(0, N_REP * CAP // 4, land_some, 0)
    tails_out[...] = tails[...].astype(bf16)
    column = jnp.broadcast_to(gain[...], (T, T)).T

    def norm(g, carry):
        for copy in load(g):
            copy.wait()
        for t in range(4):
            h = g * 4 + t
            for r in range(2):
                rows = slice(r * T, (r + 1) * T)
                value = back[h, rows, :].astype(f32)
                inverse = lax.rsqrt(jnp.mean(value * value, axis=0, keepdims=True) + 1e-6)
                z = z_in[h, rows, :].astype(f32)
                mixed_out[h, rows, :] = (value * inverse * column * (z / (1.0 + jnp.exp(-z)))).astype(bf16)
        store_mixer(g).start()
        return carry

    lax.fori_loop(0, N_SEQ // 4, norm, 0)

    def drain(h, carry):
        store_states(h).wait()
        store_mixer(h).wait()
        return carry

    lax.fori_loop(0, 4, drain, 0)


def finish_call(*operands):
    dma = pltpu.SemaphoreType.DMA
    return pl.pallas_call(
        finish_kernel,
        name="finish",
        out_shape=[
            jax.ShapeDtypeStruct((1, N_SEQ, 2 * T, T), bf16),
            jax.ShapeDtypeStruct((1, N_REP * CAP, 2, T, T), f32),
            jax.ShapeDtypeStruct((3, N_REP * CAP, 512), bf16)],
        in_specs=[HBM] * 5,
        out_specs=[HBM, HBM, VMEM],
        scratch_shapes=[
            pltpu.VMEM((N_SEQ, 2 * T, T), bf16),
            pltpu.VMEM((N_SEQ, 2 * T, T), bf16),
            pltpu.VMEM((N_REP * CAP, 2, T, T), f32),
            pltpu.VMEM((N_SEQ, 2 * T, T), bf16),
            pltpu.VMEM((1, T), f32),
            pltpu.VMEM((N_REP, CAP, 2, T, T), bf16),
            pltpu.VMEM((N_REP, 16, 512), bf16),
            pltpu.VMEM((3, N_REP * CAP, 512), f32),
            dma((4,)), dma((4,)), dma((4,)), dma((4,)), dma((3,))],
        compiler_params=pltpu.CompilerParams(vmem_limit_bytes=VMEM_GRANT),
    )(*operands)


def body(mixed, decay_in, beta_in, gate_z, conv_weight, a_log, dt_bias, norm_gain, req_blocks, replica_of, finished):
    dma = pltpu.SemaphoreType.DMA
    back, got_states, got_tails = pl.pallas_call(
        main_kernel,
        name="main",
        out_shape=[
            jax.ShapeDtypeStruct((N_SEQ, 2 * T, T), bf16),
            jax.ShapeDtypeStruct((N_REP, CAP, 2, T, T), bf16),
            jax.ShapeDtypeStruct((N_REP, 16, 512), bf16)],
        in_specs=[HBM] * 9,
        out_specs=[HBM] * 3,
        scratch_shapes=[pltpu.VMEM(*SCRATCH[name]) for name in SCRATCH_NAMES] + [
            pltpu.VMEM((N_SEQ, 8, T), f32),
            pltpu.VMEM((N_REP, CAP, 2, T, T), bf16),
            pltpu.VMEM((N_REP, 16, 512), bf16),
            pltpu.SMEM((N_REP * CAP,), jnp.int32),
            pltpu.SMEM((N_REP * CAP,), jnp.int32)] + [dma((N_SEQ,))] * 6 + [dma((N_REP,))] * 4 + [
                dma((5,)),
                pltpu.VMEM(decay_in.shape, bf16), pltpu.VMEM(beta_in.shape, bf16), pltpu.VMEM((1, 4, 512), bf16),
                pltpu.SMEM(a_log.shape, f32), pltpu.SMEM(dt_bias.shape, f32), pltpu.SMEM(req_blocks.shape, jnp.int32),
                pltpu.SMEM(replica_of.shape, jnp.int32), pltpu.SMEM(finished.shape, jnp.int32), dma((8,))],
        compiler_params=pltpu.CompilerParams(
            collective_id=0, has_side_effects=True, vmem_limit_bytes=VMEM_GRANT),
    )(mixed, decay_in, beta_in, jnp.transpose(conv_weight, (1, 0, 2)), a_log, dt_bias, req_blocks, replica_of, finished)
    mixer, states, tails = finish_call(back, gate_z, norm_gain.reshape(1, T), got_states, got_tails)
    tails = jnp.transpose(tails, (1, 0, 2))[None, :, :, None, :]
    return mixer, states, tails


def solution(mesh):
    placed = P("rep", None, None, "seq")
    return jax.shard_map(
        body,
        mesh=mesh,
        in_specs=(placed, placed, placed, placed, P(None, "seq", None), P("seq"), P("seq"), P(),
                  P("rep", None), P("rep", None), P("rep", None)),
        out_specs=(placed, P("rep", None, "seq", None, None), P("rep", None, None, "seq", None)),
        check_vma=False,
    )
```

```python
import jax
import jax.numpy as jnp
from jax import lax
from jax.experimental import pallas as pl
from jax.experimental.pallas import tpu as pltpu
from jax.sharding import PartitionSpec as P

f32, bf16 = jnp.float32, jnp.bfloat16
NC, T, SPAN = 16, 128, 64

def dot(a, b):
    return jnp.dot(a, b, preferred_element_type=f32)

def dot_nt(a, b):
    return lax.dot_general(a, b, (((1,), (1,)), ((), ())), preferred_element_type=f32)

def iota(shape, d):
    return lax.broadcasted_iota(jnp.int32, shape, d)

def setup_tables(s):
    j, i = iota((T, T), 0), iota((T, T), 1)
    same = (j // SPAN) == (i // SPAN)
    s.seen[...] = jnp.where(same & (j <= i), 1.0, 0.0)
    s.later[...] = jnp.where(same & (j < i), 1.0, 0.0)
    s.eye[...] = jnp.where(j == i, 1.0, 0.0)
    for level in range(6):
        s.level[level] = jnp.where(((j ^ i) >> level) == 1, 1.0, 0.0).astype(bf16)
    taps = s.conv_weight[...].reshape(4, 512).astype(f32)
    taps = jnp.concatenate([taps, jnp.zeros((4, 512), f32)], axis=0).T
    for tap in range(4):
        s.taps[tap] = jnp.broadcast_to(taps[:, tap:tap + 1], (512, T))
    block = iota((32, T), 0)
    start = jnp.int32(0)
    hit = jnp.zeros((32, T), f32)
    for q in range(8):
        hit = jnp.where(block == start, 1.0, hit)
        start = start + s.req_blocks[0, q]
    s.stay[...] = 1.0 - hit

def setup_gates(s):
    lane = iota((NC, T), 1)
    for r in range(2):
        x = s.aux[:, r, :] + s.dt_bias[r]
        rate = jnp.exp(jnp.full((NC, T), s.a_log[r], f32))
        decay = -rate * (jnp.maximum(x, 0.0) + jnp.log1p(jnp.exp(-jnp.abs(x))))
        c = decay
        for sh in (1, 2, 4, 8, 16, 32):
            c = c + jnp.where(lane % SPAN >= sh, pltpu.roll(c, sh, 1), 0.0)
        end0 = jnp.broadcast_to(c[:, SPAN - 1:SPAN], (NC, T))
        end1 = jnp.broadcast_to(c[:, T - 1:T], (NC, T))
        s.cum[r] = c
        s.fade[r] = jnp.exp(jnp.where(lane < SPAN, end0, end1) - c)
        s.lift[r] = jnp.exp(c)
        s.beta[r] = 1.0 / (1.0 + jnp.exp(-s.aux[:, 2 + r, :]))
        s.keep[r, 0] = jnp.exp(end0)
        s.keep[r, 1] = jnp.exp(end1)

def row(ref, c):
    return ref[pl.ds(c, 1), :]

def read_chunk(s, c):
    before = lax.rem(c + NC - 1, NC)
    lane = iota((1, T), 1)
    token = lane + c * T
    start = jnp.int32(0)
    since = token
    for q in range(7):
        start = start + s.req_blocks[0, q] * SPAN
        since = jnp.where(token >= start, token - start, since)
    now = s.x[c]
    old = s.x[before]
    parts = []
    for g in range(4):
        rows = slice(g * T, (g + 1) * T)
        cur = now[rows].astype(f32)
        prev = old[rows].astype(f32)
        total = s.taps[3, rows, :] * cur
        for back in (1, 2, 3):
            moved = pltpu.roll(jnp.where(lane >= T - back, prev, cur), back, 1)
            total = total + s.taps[3 - back, rows, :] * jnp.where(since >= back, moved, 0.0)
        parts.append((total / (1.0 + jnp.exp(-total))).astype(bf16))
    qT = parts[0]
    kw = parts[1].astype(f32)
    kT = (kw * lax.rsqrt(jnp.sum(kw * kw, axis=0, keepdims=True) + 1e-6)).astype(bf16)
    k = kT.astype(f32).T.astype(bf16)
    both = dot(k, jnp.concatenate([kT, qT], axis=1))
    gram, raw = both[:, :T], both[:, T:]
    minus = []
    for r in range(2):
        cum = row(s.cum.at[r], c)
        col = jnp.broadcast_to(cum, (T, T)).T
        e = jnp.exp((cum - col) * s.seen[...]) * s.seen[...]
        s.score[c, r] = (raw * e).astype(bf16)
        minus.append(gram * e * (s.later[...] * row(s.beta.at[r], c)))
    j, i = iota((16, T), 0), iota((16, T), 1)
    pick = jnp.where((j % 8 < 3) & (i == (j // 8) * SPAN + SPAN - 3 + j % 8), 1.0, 0.0).astype(bf16)
    tails = dot_nt(pick, now)
    s.tails[2 * c] = tails[:8]
    s.tails[2 * c + 1] = tails[8:]
    return qT, kT, k, parts[2:], minus


def solve(s, minus):
    low = [n.astype(bf16) for n in minus]
    count = range(len(minus))
    u = [(s.eye[...] - n * s.level[0].astype(f32)).astype(bf16) for n in minus]
    for level in range(1, 6):
        p = [dot(u[m], low[m] * s.level[level]).astype(bf16) for m in count]
        u = [u[m] - dot(p[m], u[m]).astype(bf16) for m in count]
    rest = [(minus[m] - low[m].astype(f32)).astype(bf16) for m in count]
    nx = [dot(jnp.concatenate([low[m], rest[m]], axis=0), u[m]) for m in count]
    res = [(s.eye[...] - u[m].astype(f32) - (nx[m][:T] + nx[m][T:])).astype(bf16) for m in count]
    return [(u[m].astype(f32) + dot(u[m], res[m])).astype(bf16) for m in count]


def weigh(s, chunks, data, u):
    zero = jnp.zeros((SPAN, T), bf16)
    pairs = [(m, r) for m in range(len(chunks)) for r in range(2)]
    kk, left, fade, stay, keep0, keep1 = [], [], [], [], [], []
    for m, c in enumerate(chunks):
        qT, kT, k, values, _ = data[m]
        kk.append(jnp.concatenate([
            jnp.concatenate([k[:SPAN], zero], axis=0),
            jnp.concatenate([zero, k[SPAN:]], axis=0)], axis=1))
        for r in range(2):
            beta = row(s.beta.at[r], c)
            sk = (kT.astype(f32) * (beta * row(s.lift.at[r], c))).astype(bf16)
            sv = (values[r].astype(f32) * beta).astype(bf16)
            left.append(jnp.concatenate([sv, sk], axis=0))
            fade.append(row(s.fade.at[r], c))
            stay.append(row(s.stay, 2 * c + 1))
            keep0.append(row(s.keep.at[r, 0], c))
            keep1.append(row(s.keep.at[r, 1], c))
    w = [dot(left[n], u[n]) for n in range(len(pairs))]
    gw = [dot((w[n] * fade[n]).astype(bf16), kk[m]) for n, (m, r) in enumerate(pairs)]
    joined = [g[:, :T].astype(bf16) for g in gw]
    both = [dot(joined[n], gw[n][T:, T:].astype(bf16)) for n in range(len(pairs))]
    for n, (m, r) in enumerate(pairs):
        c, g = chunks[m], gw[n]
        wb = w[n].astype(bf16)
        s.wv[c, r] = wb[:T]
        s.wq[c, r, :, :T] = wb[T:]
        s.wq[c, r, :, T:] = data[m][0]
        s.add[c, r, 0] = g[:T, :T]
        s.add[c, r, 1] = g[:T, T:] + stay[n] * (keep1[n] * g[:T, :T] - both[n][:T])
        s.turn[c, r, :, :T] = joined[n][T:]
        s.turn[c, r, :, T:] = (stay[n] * (keep1[n] * g[T:, :T] + keep0[n] * g[T:, T:] - both[n][T:])).astype(bf16)


def prep_chunks(s, chunks):
    data = [read_chunk(s, c) for c in chunks]
    minus = [n for d in data for n in d[4]]
    u = solve(s, minus)
    weigh(s, chunks, data, u)

def scan_blocks(s):
    def step(c, carry):
        state = list(carry)
        stay0, stay1 = row(s.stay, 2 * c), row(s.stay, 2 * c + 1)
        for r in range(2):
            keep0, keep1 = row(s.keep.at[r, 0], c), row(s.keep.at[r, 1], c)
            inside = state[r] * stay0
            low = inside.astype(bf16)
            moved = dot(low, s.turn[c, r])
            state[r] = (stay1 * keep0 * keep1 * inside + s.add[c, r, 1]) - moved[:, T:]
            middle = (keep0 * inside + s.add[c, r, 0]) - moved[:, :T]
            s.enter[c, r, :T, :] = low
            s.enter[c, r, T:, :] = (middle * stay1).astype(bf16)
            s.leave[2 * c, r] = middle.astype(bf16)
            s.leave[2 * c + 1, r] = state[r].astype(bf16)
        return tuple(state)

    zero = jnp.zeros((T, T), f32)
    lax.fori_loop(0, NC, step, (zero, zero))


def post_chunks(s, chunks):
    first = iota((1, T), 1) < SPAN
    pairs = [(c, r) for c in chunks for r in range(2)]
    both = [dot(s.enter[c, r], s.wq[c, r]) for c, r in pairs]
    new = [(s.wv[c, r].astype(f32) - jnp.where(first, x[:T, :T], x[T:, :T])).astype(bf16)
           for (c, r), x in zip(pairs, both)]
    old = [row(s.lift.at[r], c) * jnp.where(first, x[:T, T:], x[T:, T:]) for (c, r), x in zip(pairs, both)]
    out = [(old[n] + dot(new[n], s.score[c, r])).astype(bf16) for n, (c, r) in enumerate(pairs)]
    for n, (c, r) in enumerate(pairs):
        s.core[c, r * T:(r + 1) * T, :] = out[n]


SCRATCH = dict(
    x=((NC, 512, T), bf16), aux=((NC, 8, T), f32),
    cum=((2, NC, T), f32), fade=((2, NC, T), f32), lift=((2, NC, T), f32), beta=((2, NC, T), f32),
    keep=((2, 2, NC, T), f32), stay=((32, T), f32),
    seen=((T, T), f32), later=((T, T), f32), eye=((T, T), f32), level=((6, T, T), bf16),
    taps=((4, 512, T), f32),
    wv=((NC, 2, T, T), bf16), wq=((NC, 2, T, 2 * T), bf16), score=((NC, 2, T, T), bf16),
    add=((NC, 2, 2, T, T), f32), turn=((NC, 2, T, 2 * T), bf16),
    enter=((NC, 2, 2 * T, T), bf16), leave=((32, 2, T, T), bf16),
    core=((NC, 256, T), bf16), tails=((32, 8, 512), f32),
)

class Refs:
    pass


N_SEQ, N_REP, REQS, CAP = 16, 8, 8, 2
AHEAD = 11
BEFORE = 2
FIRST = False
VMEM_GRANT = 63 << 20
MESH = pl.DeviceIdType.MESH
VMEM = pl.BlockSpec(memory_space=pltpu.VMEM)
SMEM = pl.BlockSpec(memory_space=pltpu.SMEM)
HBM = pl.BlockSpec(memory_space=pltpu.MemorySpace.HBM)
SCRATCH_NAMES = list(SCRATCH)


def fill_slots(s):
    keys, lasts = [], []
    last = jnp.int32(-1)
    for q in range(REQS):
        last = last + s.req_blocks[0, q]
        rank = jnp.int32(0)
        for p in range(q):
            hit = (s.replica_of[0, p] == s.replica_of[0, q]) & (s.finished[0, p] > 0)
            rank = rank + jnp.where(hit, 1, 0)
        keys.append(jnp.where(s.finished[0, q] > 0, s.replica_of[0, q] * CAP + rank, -1))
        lasts.append(last)
    for m in range(N_REP * CAP):
        where, used = jnp.int32(0), jnp.int32(0)
        for q in range(REQS):
            where = where + jnp.where(keys[q] == m, lasts[q], 0)
            used = used + jnp.where(keys[q] == m, 1, 0)
        s.slot_block[m] = where
        s.slot_used[m] = used


def build_slot(s, d, k):
    m = d * CAP + k
    block, used = s.slot_block[m], s.slot_used[m].astype(f32)
    for r in range(2):
        flipped = dot_nt(s.eye[...].astype(bf16), s.leave[block, r])
        s.out_states[d, k, r] = (flipped * used).astype(bf16)
    count = (s.slot_used[d * CAP] + s.slot_used[d * CAP + 1]).astype(f32)
    rows = s.tails[block] * used
    return jnp.where(iota((8, 512), 0) == 3, count, rows)


ORDER = (1, 15, 4, 12, 5, 11, 3, 13, 2, 14, 8, 6, 10, 7, 9)
GROUPS = ((1, 0, 5, 12), (4, 13, 2, 15), (3, 14, 6, 11), (7, 10, 8, 9))
READY = (0, 6, 10, 13, 15)
REP_ORDER = (2, 6, 1, 7, 3, 5, 4, 0)


def entry(table, i):
    out = jnp.int32(table[0])
    for t in range(1, len(table)):
        out = jnp.where(i == t, table[t], out)
    return out


def main_kernel(mixed, decay_in, beta_in, conv_weight, a_log, dt_bias, req_blocks, replica_of, finished,
                back, got_states, got_tails, *scratch):
    s = Refs()
    names = SCRATCH_NAMES + [
        "aux_out", "out_states", "out_tails", "slot_block", "slot_used",
        "x_send", "x_recv", "aux_send", "aux_recv", "core_send", "core_recv",
        "st_send", "st_recv", "tl_send", "tl_recv", "own",
        "decay_in", "beta_in", "conv_weight", "a_log", "dt_bias", "req_blocks", "replica_of", "finished", "small"]
    for name, ref in zip(names, scratch):
        setattr(s, name, ref)
    me, rep = lax.axis_index("seq"), lax.axis_index("rep")

    barrier = pltpu.get_barrier_semaphore()
    for k in range(1, N_SEQ):
        pl.semaphore_signal(barrier, inc=1, device_id={"seq": lax.rem(me + k, N_SEQ)}, device_id_type=MESH)
    for k in range(1, N_REP):
        pl.semaphore_signal(barrier, inc=1, device_id={"rep": lax.rem(rep + k, N_REP)}, device_id_type=MESH)
    small = [
        pltpu.make_async_copy(source, target, s.small.at[n]) for n, (source, target) in enumerate((
            (decay_in, s.decay_in), (beta_in, s.beta_in), (conv_weight, s.conv_weight), (a_log, s.a_log),
            (dt_bias, s.dt_bias), (req_blocks, s.req_blocks), (replica_of, s.replica_of), (finished, s.finished)))]
    for copy in small:
        copy.start()
    own_x = pltpu.make_async_copy(mixed.at[0, me], s.x.at[me], s.own.at[0])
    own_x.start()

    def aux_copy(k):
        to = lax.rem(me + N_SEQ - k, N_SEQ)
        return pltpu.make_async_remote_copy(
            src_ref=s.aux_out.at[to], dst_ref=s.aux.at[me], send_sem=s.aux_send.at[k], recv_sem=s.aux_recv.at[k],
            device_id={"seq": to}, device_id_type=MESH)

    def x_copy(k):
        to = lax.rem(me + N_SEQ - k, N_SEQ)
        return pltpu.make_async_remote_copy(
            src_ref=mixed.at[0, to], dst_ref=s.x.at[me], send_sem=s.x_send.at[k], recv_sem=s.x_recv.at[k],
            device_id={"seq": to}, device_id_type=MESH)

    def start_aux(k, carry):
        aux_copy(k).start()
        return carry

    pl.semaphore_wait(barrier, N_SEQ + N_REP - 2)
    for n in range(BEFORE):
        x_copy(ORDER[n]).start()
    for copy in small:
        copy.wait()
    for h in range(N_SEQ):
        s.aux_out[h, 0:2, :] = s.decay_in[0, h].astype(f32)
        s.aux_out[h, 2:4, :] = s.beta_in[0, h].astype(f32)
        s.aux_out[h, 4:8, :] = jnp.zeros((4, T), f32)

    own_aux = pltpu.make_async_copy(s.aux_out.at[me], s.aux.at[me], s.own.at[1])
    own_aux.start()
    lax.fori_loop(1, N_SEQ, start_aux, 0)
    for n in range(BEFORE, AHEAD):
        x_copy(ORDER[n]).start()
    setup_tables(s)
    fill_slots(s)
    own_x.wait()
    own_aux.wait()

    def wait_aux(k, carry):
        aux_copy(k).wait_recv()
        return carry

    lax.fori_loop(1, N_SEQ, wait_aux, 0)
    setup_gates(s)

    def prep(g, carry):
        for n in range(4):
            @pl.when(g == n)
            def _(n=n):
                for m in range(READY[n], READY[n + 1]):
                    x_copy(ORDER[m]).wait_recv()
                    if m + AHEAD < N_SEQ - 1:
                        x_copy(ORDER[m + AHEAD]).start()

        prep_chunks(s, [lax.rem(me + entry([group[t] for group in GROUPS], g), N_SEQ) for t in range(4)])
        return carry

    lax.fori_loop(0, 4, prep, 0)
    scan_blocks(s)

    def core_copy(k):
        to = lax.rem(me + k, N_SEQ)
        return pltpu.make_async_remote_copy(
            src_ref=s.core.at[to], dst_ref=back.at[me], send_sem=s.core_send.at[k], recv_sem=s.core_recv.at[k],
            device_id={"seq": to}, device_id_type=MESH)

    def state_copies(k):
        to = lax.rem(rep + k, N_REP)
        return [
            pltpu.make_async_remote_copy(
                src_ref=s.out_states.at[to], dst_ref=got_states.at[rep], send_sem=s.st_send.at[k],
                recv_sem=s.st_recv.at[k], device_id={"rep": to}, device_id_type=MESH),
            pltpu.make_async_remote_copy(
                src_ref=s.out_tails.at[to], dst_ref=got_tails.at[rep], send_sem=s.tl_send.at[k],
                recv_sem=s.tl_recv.at[k], device_id={"rep": to}, device_id_type=MESH)]

    def hand_off(g):
        for t in range(2):
            k = entry([REP_ORDER[2 * n + t] for n in range(4)], g)
            d = lax.rem(rep + k, N_REP)
            tails = [build_slot(s, d, slot) for slot in range(CAP)]
            s.out_tails[d] = jnp.concatenate(tails, axis=0).astype(bf16)

            @pl.when(k > 0)
            def _(k=k):
                for copy in state_copies(k):
                    copy.start()

    def post(g, carry):
        steps = [entry([(ORDER + (0,))[4 * n + t] for n in range(4)], g) for t in range(4)]
        post_chunks(s, [lax.rem(me + k, N_SEQ) for k in steps])
        for t in range(4):
            @pl.when(steps[t] > 0)
            def _(t=t):
                core_copy(steps[t]).start()

        if not FIRST:
            hand_off(g)
        return carry

    def hand_off_first(g, carry):
        hand_off(g)
        return carry

    if FIRST:
        lax.fori_loop(0, 4, hand_off_first, 0)
    lax.fori_loop(0, 4, post, 0)
    own = [
        pltpu.make_async_copy(s.core.at[me], back.at[me], s.own.at[2]),
        pltpu.make_async_copy(s.out_states.at[rep], got_states.at[rep], s.own.at[3]),
        pltpu.make_async_copy(s.out_tails.at[rep], got_tails.at[rep], s.own.at[4])]
    for copy in own:
        copy.start()

    def finish_seq(k, carry):
        aux_copy(k).wait_send()
        x_copy(k).wait_send()
        core_copy(k).wait()
        return carry

    def finish_rep(k, carry):
        for copy in state_copies(k):
            copy.wait()
        return carry

    lax.fori_loop(1, N_SEQ, finish_seq, 0)
    lax.fori_loop(1, N_REP, finish_rep, 0)
    for copy in own:
        copy.wait()


def finish_kernel(back_hbm, gate, gain_hbm, got_states_hbm, got_tails_hbm, mixer, states, tails_out,
                  z_in, mixed_out, states_out, back, gain, got_states, got_tails, tails,
                  gate_sem, back_sem, mixer_sem, states_sem, load_sem):
    first = [
        pltpu.make_async_copy(got_tails_hbm, got_tails, load_sem.at[0]),
        pltpu.make_async_copy(got_states_hbm, got_states, load_sem.at[1]),
        pltpu.make_async_copy(gain_hbm, gain, load_sem.at[2])]

    def some(g):
        return pl.ds(4 * g, 4)

    def load(g):
        return [
            pltpu.make_async_copy(gate.at[0, some(g)], z_in.at[some(g)], gate_sem.at[g]),
            pltpu.make_async_copy(back_hbm.at[some(g)], back.at[some(g)], back_sem.at[g])]

    for copy in first:
        copy.start()
    for g in range(4):
        for copy in load(g):
            copy.start()
    for copy in first:
        copy.wait()
    counts = [jnp.max(got_tails[q, 0:8, 0:T].astype(f32)[3:4]).astype(jnp.int32) for q in range(N_REP)]
    bases, base = [], jnp.int32(0)
    for q in range(N_REP):
        bases.append(base)
        base = base + counts[q]

    def store_states(g):
        return pltpu.make_async_copy(states_out.at[some(g)], states.at[0, some(g)], states_sem.at[g])

    def store_mixer(g):
        return pltpu.make_async_copy(mixed_out.at[some(g)], mixer.at[0, some(g)], mixer_sem.at[g])

    def land(slot):
        pick, used = jnp.int32(0), jnp.int32(0)
        for q in range(N_REP):
            rank = slot - bases[q]
            hit = (rank >= 0) & (rank < counts[q])
            pick = jnp.where(hit, q * CAP + rank, pick)
            used = jnp.where(hit, 1, used)
        scale = used.astype(f32)
        source, rank = pick // CAP, pick % CAP
        for r in range(2):
            states_out[slot, r] = got_states[source, rank, r].astype(f32) * scale
        both = got_tails[source].astype(f32)
        rows = jnp.where(rank == 0, both[0:8], both[8:16]) * scale
        for p in range(3):
            tails[p, pl.ds(slot, 1), :] = rows[p:p + 1]

    def land_some(g, carry):
        for t in range(4):
            land(g * 4 + t)
        store_states(g).start()
        return carry

    lax.fori_loop(0, N_REP * CAP // 4, land_some, 0)
    tails_out[...] = tails[...].astype(bf16)
    column = jnp.broadcast_to(gain[...], (T, T)).T

    def norm(g, carry):
        for copy in load(g):
            copy.wait()
        for t in range(4):
            h = g * 4 + t
            for r in range(2):
                rows = slice(r * T, (r + 1) * T)
                value = back[h, rows, :].astype(f32)
                inverse = lax.rsqrt(jnp.mean(value * value, axis=0, keepdims=True) + 1e-6)
                z = z_in[h, rows, :].astype(f32)
                mixed_out[h, rows, :] = (value * inverse * column * (z / (1.0 + jnp.exp(-z)))).astype(bf16)
        store_mixer(g).start()
        return carry

    lax.fori_loop(0, N_SEQ // 4, norm, 0)

    def drain(h, carry):
        store_states(h).wait()
        store_mixer(h).wait()
        return carry

    lax.fori_loop(0, 4, drain, 0)


def finish_call(*operands):
    dma = pltpu.SemaphoreType.DMA
    return pl.pallas_call(
        finish_kernel,
        name="finish",
        out_shape=[
            jax.ShapeDtypeStruct((1, N_SEQ, 2 * T, T), bf16),
            jax.ShapeDtypeStruct((1, N_REP * CAP, 2, T, T), f32),
            jax.ShapeDtypeStruct((3, N_REP * CAP, 512), bf16)],
        in_specs=[HBM] * 5,
        out_specs=[HBM, HBM, VMEM],
        scratch_shapes=[
            pltpu.VMEM((N_SEQ, 2 * T, T), bf16),
            pltpu.VMEM((N_SEQ, 2 * T, T), bf16),
            pltpu.VMEM((N_REP * CAP, 2, T, T), f32),
            pltpu.VMEM((N_SEQ, 2 * T, T), bf16),
            pltpu.VMEM((1, T), f32),
            pltpu.VMEM((N_REP, CAP, 2, T, T), bf16),
            pltpu.VMEM((N_REP, 16, 512), bf16),
            pltpu.VMEM((3, N_REP * CAP, 512), f32),
            dma((4,)), dma((4,)), dma((4,)), dma((4,)), dma((3,))],
        compiler_params=pltpu.CompilerParams(vmem_limit_bytes=VMEM_GRANT),
    )(*operands)


def body(mixed, decay_in, beta_in, gate_z, conv_weight, a_log, dt_bias, norm_gain, req_blocks, replica_of, finished):
    dma = pltpu.SemaphoreType.DMA
    back, got_states, got_tails = pl.pallas_call(
        main_kernel,
        name="main",
        out_shape=[
            jax.ShapeDtypeStruct((N_SEQ, 2 * T, T), bf16),
            jax.ShapeDtypeStruct((N_REP, CAP, 2, T, T), bf16),
            jax.ShapeDtypeStruct((N_REP, 16, 512), bf16)],
        in_specs=[HBM] * 9,
        out_specs=[HBM] * 3,
        scratch_shapes=[pltpu.VMEM(*SCRATCH[name]) for name in SCRATCH_NAMES] + [
            pltpu.VMEM((N_SEQ, 8, T), f32),
            pltpu.VMEM((N_REP, CAP, 2, T, T), bf16),
            pltpu.VMEM((N_REP, 16, 512), bf16),
            pltpu.SMEM((N_REP * CAP,), jnp.int32),
            pltpu.SMEM((N_REP * CAP,), jnp.int32)] + [dma((N_SEQ,))] * 6 + [dma((N_REP,))] * 4 + [
                dma((5,)),
                pltpu.VMEM(decay_in.shape, bf16), pltpu.VMEM(beta_in.shape, bf16), pltpu.VMEM((1, 4, 512), bf16),
                pltpu.SMEM(a_log.shape, f32), pltpu.SMEM(dt_bias.shape, f32), pltpu.SMEM(req_blocks.shape, jnp.int32),
                pltpu.SMEM(replica_of.shape, jnp.int32), pltpu.SMEM(finished.shape, jnp.int32), dma((8,))],
        compiler_params=pltpu.CompilerParams(
            collective_id=0, has_side_effects=True, vmem_limit_bytes=VMEM_GRANT),
    )(mixed, decay_in, beta_in, jnp.transpose(conv_weight, (1, 0, 2)), a_log, dt_bias, req_blocks, replica_of, finished)
    mixer, states, tails = finish_call(back, gate_z, norm_gain.reshape(1, T), got_states, got_tails)
    tails = jnp.transpose(tails, (1, 0, 2))[None, :, :, None, :]
    return mixer, states, tails


def solution(mesh):
    placed = P("rep", None, None, "seq")
    return jax.shard_map(
        body,
        mesh=mesh,
        in_specs=(placed, placed, placed, placed, P(None, "seq", None), P("seq"), P("seq"), P(),
                  P("rep", None), P("rep", None), P("rep", None)),
        out_specs=(placed, P("rep", None, "seq", None, None), P("rep", None, None, "seq", None)),
        check_vma=False,
    )
```
